32 devices in a mesh: dp: 4 (over y, x), segment: 4 (over z), mp: 2 (over core).
Axes of the slice: x: 2, y: 2, z: 4, core: 2. Of those that a mesh axis runs over, the one named last changes fastest.
Arguments:
- trunk_in: bfloat16 [1024, 2560], P('dp', 'mp'), may hold values from -6 to 6
- norm_gain: bfloat16 [4, 2560], P('segment'), may hold values from 0.5 to 1.5
- w_gate: bfloat16 [4, 2560, 3584], P('segment', 'dp', 'mp'), may hold values from -0.125 to 0.125
- w_up: bfloat16 [4, 2560, 3584], P('segment', 'dp', 'mp'), may hold values from -0.125 to 0.125
- w_down: bfloat16 [4, 3584, 2560], P('segment', 'mp', 'dp'), may hold values from -0.09375 to 0.09375
- w_cond: bfloat16 [2560, 512], P('mp'), may hold values from -0.125 to 0.125
- w_time: bfloat16 [256, 512], replicated, may hold values from -0.375 to 0.375
- w_in: bfloat16 [70, 256], replicated, may hold values from -0.75 to 0.75
- w_mid: bfloat16 [1280, 256], replicated, may hold values from -0.15625 to 0.15625
- w_res: bfloat16 [14, 256], replicated, may hold values from -1.5 to 1.5
- w_out: bfloat16 [256, 14], replicated, may hold values from -0.375 to 0.375
- tsteps: int32 [64, 8], P('dp'), may hold values from 0 to 99
- advantage: float32 [64, 8], P('dp'), may hold values from -4 to 4
- actions: bfloat16 [64, 64, 14], P('dp'), may hold values from -6 to 6
- noise: bfloat16 [64, 8, 64, 14], P('dp'), may hold values from -6 to 6
Outputs:
- grad_w_in: float32 [70, 256], P(None, 'segment')
- grad_w_mid: float32 [1280, 256], P(None, 'segment')
- grad_w_res: float32 [14, 256], P(None, 'segment')
- grad_w_out: float32 [256, 14], P('segment')
- grad_w_time: float32 [256, 512], P(None, 'segment')
- grad_w_cond: float32 [2560, 512], P('mp', 'segment')
- grad_cond: float32 [64, 2560], P(('dp', 'segment'), 'mp')
- loss: float32 [1], replicated
The draws below stay inside these ranges and needn't reach their ends.
All inputs are finite; a program needn't handle non-finite values.
Results may differ from the reference program's by a relative error of at most 0.035.
Values may be sent and summed in bfloat16 or wider, within the bound.
No kernel may reach another device: no remote copies, remote signals or barrier semaphores. Data moves between devices by JAX's collectives and lax.ppermute only.
A program may use at most 128 MiB of HBM per device.

```python
import math
import jax
import jax.numpy as jnp
from jax import lax

D = 2560
FF = 3584
C = 256
DSED = 256
H = 64
A = 14
GROUPS = 8
TSTEPS = 100
TPS = 16
SPD = 16
LEV = 8
SAMPLES = 64
TOKENS = 1024
N_DP = 4
N_SEGMENT = 4


def plant(values, own_key, least, largest):
    longest = values.shape.index(max(values.shape))
    spots = []
    for shift in (0, 1):
        where = [jax.random.randint(jax.random.fold_in(own_key, axis), (), 0, length) for axis, length in enumerate(values.shape)]
        where[longest] = (where[longest] + shift) % values.shape[longest]
        spots.append(tuple(where))
    return values.at[spots[0]].set(least).at[spots[1]].set(largest)


def block_levels(stream_key, shape, cuts, least, top_value):
    def one(axis_at, shards_of):
        steps = jax.random.uniform(jax.random.fold_in(jax.random.fold_in(stream_key, 6), axis_at), (shards_of,), jnp.float32, least / len(cuts), top_value / len(cuts))
        return jnp.repeat(jnp.exp(steps), shape[axis_at] // shards_of).reshape((-1,) + (1,) * (len(shape) - axis_at - 1))

    gain = one(*cuts[0])
    for cut in cuts[1:]:
        gain = gain * one(*cut)
    return gain


def centred(rng, dims, deviation, most, shards=(), kind=jnp.bfloat16):
    level = block_levels(rng, dims, shards, -0.22, 0.18) if shards else 1.0
    entries = jax.random.normal(rng, dims, jnp.float32) * deviation * level
    return jnp.minimum(jnp.maximum(entries, -most), most).astype(kind)


def setup_inputs(seed: int = 0) -> dict:
    seeds = jax.random.split(jax.random.key(seed), 16)
    trunk_in = centred(seeds[0], (TOKENS, D), 1.0, 6.0, ((0, 4), (1, 2)))
    norm_gain = jnp.clip(1.0 + 0.1 * jax.random.normal(seeds[1], (N_SEGMENT, D), jnp.float32), 0.5, 1.5).astype(jnp.bfloat16)
    w_gate = centred(seeds[2], (N_SEGMENT, D, FF), D ** -0.5, 0.125, ((0, 4), (1, 4), (2, 2)))
    w_up = centred(seeds[3], (N_SEGMENT, D, FF), D ** -0.5, 0.125, ((0, 4), (1, 4), (2, 2)))
    w_down = centred(seeds[4], (N_SEGMENT, FF, D), FF ** -0.5, 0.09375, ((0, 4), (1, 2), (2, 4)))
    w_cond = centred(seeds[5], (D, 2 * C), D ** -0.5, 0.125, ((0, 2),))
    w_time = centred(seeds[6], (DSED, 2 * C), DSED ** -0.5, 0.375)
    w_in = centred(seeds[7], (5 * A, C), (5 * A) ** -0.5, 0.75)
    w_mid = centred(seeds[8], (5 * C, C), (5 * C) ** -0.5, 0.15625)
    w_res = centred(seeds[9], (A, C), A ** -0.5, 1.5)
    w_out = centred(seeds[10], (C, A), C ** -0.5, 0.375)
    tsteps = plant(jax.random.randint(seeds[11], (SAMPLES, LEV), 0, TSTEPS), jax.random.fold_in(seeds[11], 1), 0, TSTEPS - 1).astype(jnp.int32)
    advantage = centred(seeds[12], (SAMPLES, LEV), 1.0, 4.0, ((0, 4),), jnp.float32)
    actions = centred(seeds[13], (SAMPLES, H, A), 1.0, 6.0, ((0, 4),))
    noise = centred(seeds[14], (SAMPLES, LEV, H, A), 1.0, 6.0, ((0, 4),))
    return {"trunk_in": trunk_in, "norm_gain": norm_gain, "w_gate": w_gate, "w_up": w_up, "w_down": w_down, "w_cond": w_cond, "w_time": w_time, "w_in": w_in, "w_mid": w_mid, "w_res": w_res, "w_out": w_out, "tsteps": tsteps, "advantage": advantage, "actions": actions, "noise": noise}


def mish_value(values):
    return values * jnp.tanh(jax.nn.softplus(values))

def mish_slope(values):
    soft = jnp.tanh(jax.nn.softplus(values))
    return soft + values * jax.nn.sigmoid(values) * (1.0 - soft * soft)

def contract(form, left, right):
    return jnp.einsum(form, left.astype(jnp.float32), right.astype(jnp.float32))

def alpha_table():
    grid = jnp.arange(TSTEPS + 1, dtype=jnp.float32) / TSTEPS
    curve = jnp.cos((grid + 0.008) / 1.008 * math.pi / 2.0) ** 2
    betas = jnp.minimum(1.0 - curve[1:] / curve[:-1], 0.999)
    return jnp.cumprod(1.0 - betas)

def norm_act(values):
    rows, steps, channels = values.shape
    grouped = values.reshape(rows, steps, GROUPS, channels // GROUPS)
    center = lax.optimization_barrier(jnp.mean(grouped, axis=(1, 3), keepdims=True))
    spread = lax.optimization_barrier(jnp.mean((grouped - center) ** 2, axis=(1, 3), keepdims=True))
    normed = (grouped - center) * lax.rsqrt(spread + 1e-05)
    return mish_value(normed.reshape(rows, steps, channels))

def columns(values):
    steps = values.shape[1]
    padded = jnp.pad(values, ((0, 0), (2, 2), (0, 0)))
    return jnp.concatenate([padded[:, tap:tap + steps] for tap in range(5)], axis=2)

def columns_adjoint(grads, width):
    total = 0.0
    for tap in range(5):
        piece = grads[:, :, tap * width:(tap + 1) * width]
        total = total + jnp.pad(piece, ((0, 0), (tap, 4 - tap), (0, 0)))
    return total[:, 2:-2]

def denoise(film_cond, tsteps, advantage, actions, noise, w_in, w_mid, w_res, w_out, w_time, product):
    row_count, levels = tsteps.shape
    horizon, action_dims = (actions.shape[1], actions.shape[2])
    channels = w_mid.shape[1]
    flat = row_count * levels
    matches = (tsteps[:, :, None] == jnp.arange(TSTEPS, dtype=jnp.int32)[None, None, :]).astype(jnp.float32)
    alpha = lax.optimization_barrier(jnp.sum(matches * alpha_table()[None, None, :], axis=2))
    keep_root = jnp.sqrt(alpha)[:, :, None, None]
    noise_root = jnp.sqrt(1.0 - alpha)[:, :, None, None]
    noisy_act = (keep_root * actions.astype(jnp.float32)[:, None] + noise_root * noise.astype(jnp.float32)).astype(jnp.bfloat16)
    noisy_act = noisy_act.reshape(flat, horizon, action_dims)
    half_dim = w_time.shape[0] // 2
    frequencies = jnp.exp(-math.log(10000.0) * jnp.arange(half_dim, dtype=jnp.float32) / (half_dim - 1))
    angles = tsteps.astype(jnp.float32)[:, :, None] * frequencies[None, None, :]
    embedded = jnp.concatenate([jnp.sin(angles), jnp.cos(angles)], axis=2)
    time_act = mish_value(embedded).astype(jnp.bfloat16).reshape(flat, 2 * half_dim)
    film = film_cond[:, None, :] + product('rld,dc->rlc', time_act.reshape(row_count, levels, -1), w_time)
    film = film.reshape(flat, 2 * channels)
    film_scale = film[:, None, :channels]
    film_shift = film[:, None, channels:]
    columns_in = columns(noisy_act)
    pre_first = product('mhk,kc->mhc', columns_in, w_in)
    act_first, first_back = jax.vjp(norm_act, pre_first)
    modulated = (film_scale * act_first + film_shift).astype(jnp.bfloat16)
    columns_mid = columns(modulated)
    pre_second = product('mhk,kc->mhc', columns_mid, w_mid)
    act_second, second_back = jax.vjp(norm_act, pre_second)
    block_out = (act_second + product('mha,ac->mhc', noisy_act, w_res)).astype(jnp.bfloat16)
    predicted = product('mhc,ca->mha', block_out, w_out)
    errors = predicted - noise.reshape(flat, horizon, action_dims).astype(jnp.float32)
    err_sum = jnp.sum(errors * errors) / (horizon * action_dims)
    weights = advantage.reshape(flat, 1, 1)
    d_pred = (2.0 * weights * errors / (horizon * action_dims)).astype(jnp.bfloat16)
    grad_out = product('mhc,mha->ca', block_out, d_pred)
    d_block = product('mha,ca->mhc', d_pred, w_out)
    grad_res = product('mha,mhc->ac', noisy_act, d_block.astype(jnp.bfloat16))
    d_second = second_back(d_block)[0].astype(jnp.bfloat16)
    grad_mid = product('mhk,mhc->kc', columns_mid, d_second)
    d_columns = product('mhc,kc->mhk', d_second, w_mid)
    d_modulated = columns_adjoint(d_columns, channels)
    d_film = jnp.concatenate([lax.optimization_barrier(jnp.sum(d_modulated * act_first, axis=1)), lax.optimization_barrier(jnp.sum(d_modulated, axis=1))], axis=1)
    d_first = first_back(film_scale * d_modulated)[0].astype(jnp.bfloat16)
    grad_in = product('mhk,mhc->kc', columns_in, d_first)
    grad_time = product('md,mc->dc', time_act, d_film.astype(jnp.bfloat16))
    d_film_cond = lax.optimization_barrier(jnp.sum(d_film.reshape(row_count, levels, -1), axis=1))
    return (err_sum, grad_in, grad_mid, grad_res, grad_out, grad_time, d_film_cond)

def reference(trunk_in, norm_gain, w_gate, w_up, w_down, w_cond, w_time, w_in, w_mid, w_res, w_out, tsteps, advantage, actions, noise):
    hidden_state = trunk_in
    for section in range(N_SEGMENT):
        widened = hidden_state.astype(jnp.float32)
        factor = lax.rsqrt(lax.optimization_barrier(jnp.mean(widened * widened, axis=1, keepdims=True)) + 1e-05)
        normed = (widened * factor * norm_gain[section].astype(jnp.float32)).astype(jnp.bfloat16)
        gate_out = jnp.dot(normed, w_gate[section], preferred_element_type=jnp.float32)
        up_out = jnp.dot(normed, w_up[section], preferred_element_type=jnp.float32)
        hidden = (jax.nn.silu(gate_out) * up_out).astype(jnp.bfloat16)
        hidden_state = (widened + jnp.dot(hidden, w_down[section], preferred_element_type=jnp.float32)).astype(jnp.bfloat16)
    cond = lax.optimization_barrier(jnp.mean(hidden_state.reshape(SAMPLES, TPS, D).astype(jnp.float32), axis=1)).astype(jnp.bfloat16)
    cond_act = mish_value(cond.astype(jnp.float32)).astype(jnp.bfloat16)
    film_cond = jnp.dot(cond_act, w_cond, preferred_element_type=jnp.float32)

    def per_group(pieces):
        return denoise(pieces[0], pieces[1], pieces[2], pieces[3], pieces[4], w_in, w_mid, w_res, w_out, w_time, contract)
    grouped = (film_cond.reshape(N_DP, SPD, -1), tsteps.reshape(N_DP, SPD, LEV), advantage.reshape(N_DP, SPD, LEV), actions.reshape(N_DP, SPD, H, A), noise.reshape(N_DP, SPD, LEV, H, A))
    outcome = lax.map(per_group, grouped)
    err_sum = jnp.sum(outcome[0])
    grad_w_in = lax.optimization_barrier(jnp.sum(outcome[1], axis=0))
    grad_w_mid = lax.optimization_barrier(jnp.sum(outcome[2], axis=0))
    grad_w_res = lax.optimization_barrier(jnp.sum(outcome[3], axis=0))
    grad_w_out = lax.optimization_barrier(jnp.sum(outcome[4], axis=0))
    grad_w_time = lax.optimization_barrier(jnp.sum(outcome[5], axis=0))
    d_film_cond = outcome[6].reshape(SAMPLES, -1).astype(jnp.bfloat16)
    grad_w_cond = contract('sd,sc->dc', cond_act, d_film_cond)
    grad_cond = contract('sc,dc->sd', d_film_cond, w_cond) * mish_slope(cond.astype(jnp.float32))
    loss = (err_sum / (SAMPLES * LEV)).reshape(1)
    return (grad_w_in, grad_w_mid, grad_w_res, grad_w_out, grad_w_time, grad_w_cond, grad_cond, loss)
```

```python
import functools
import math

import jax
import jax.numpy as jnp
from jax import lax
from jax.experimental import pallas as pl
from jax.experimental.pallas import tpu as pltpu
from jax.sharding import PartitionSpec as P

GROUPS = 8
TSTEPS = 100
LAG = 2
REPEAT = 1
DIRECT = 4
LANES = 128
VMEM_LIMIT = 32 * 2**20


def swap(value, axis, distance):
    size = lax.axis_size(axis)
    return lax.ppermute(value, axis, [(i, i ^ distance) for i in range(size)])


def hop(value, axis):
    return lax.ppermute(value, axis, [(i, i + 1) for i in range(lax.axis_size(axis) - 1)])


def few(axis):
    return lax.axis_size(axis) <= DIRECT


def gather(value, axis):
    if few(axis):
        return [value] + [swap(value, axis, k) for k in range(1, lax.axis_size(axis))]
    stacked = lax.all_gather(value, axis, axis=0, tiled=True)
    return [stacked]


def everywhere(value, axes):
    size = math.prod(lax.axis_size(axis) for axis in axes)
    sent = jnp.broadcast_to(value[None], (size,) + value.shape)
    got = lax.all_to_all(sent, axes, 0, 0, tiled=True)
    return got.reshape((-1,) + value.shape[1:])


def scatter_sum(value, axis, dim):
    size = lax.axis_size(axis)
    width = value.shape[dim] // size
    index = lax.axis_index(axis)
    if not few(axis):
        sent = jnp.stack(jnp.split(value.astype(jnp.bfloat16), size, axis=dim))
        got = lax.all_to_all(sent, axis, 0, 0, tiled=True)
        return jnp.sum(got.astype(jnp.float32), axis=0)
    total = lax.dynamic_slice_in_dim(value, index * width, width, dim)
    for k in range(1, size):
        piece = lax.dynamic_slice_in_dim(value, (index ^ k) * width, width, dim)
        total = total + swap(piece.astype(jnp.bfloat16), axis, k).astype(jnp.float32)
    return total


def mish_value(values):
    return values * jnp.tanh(jax.nn.softplus(values))


def mish_slope(values):
    soft = jnp.tanh(jax.nn.softplus(values))
    return soft + values * jax.nn.sigmoid(values) * (1.0 - soft * soft)


def contract(form, left, right):
    return jnp.einsum(form, left, right, preferred_element_type=jnp.float32)


def alpha_table():
    grid = jnp.arange(TSTEPS + 1, dtype=jnp.float32) / TSTEPS
    curve = jnp.cos((grid + 0.008) / 1.008 * math.pi / 2.0) ** 2
    betas = jnp.minimum(1.0 - curve[1:] / curve[:-1], 0.999)
    return jnp.cumprod(1.0 - betas)


def columns(values):
    steps = values.shape[1]
    padded = jnp.pad(values, ((0, 0), (2, 2), (0, 0)))
    return jnp.concatenate([padded[:, tap : tap + steps] for tap in range(5)], axis=2)


def prepare(tsteps, advantage, actions, noise, w_time):
    row_count, levels = tsteps.shape
    horizon, action_dims = (actions.shape[1], actions.shape[2])
    flat = row_count * levels
    matches = (tsteps[:, :, None] == jnp.arange(TSTEPS, dtype=jnp.int32)[None, None, :]).astype(
        jnp.float32
    )
    alpha = jnp.sum(matches * alpha_table()[None, None, :], axis=2)
    keep_root = jnp.sqrt(alpha)[:, :, None, None]
    noise_root = jnp.sqrt(1.0 - alpha)[:, :, None, None]
    noisy_act = (
        keep_root * actions.astype(jnp.float32)[:, None] + noise_root * noise.astype(jnp.float32)
    ).astype(jnp.bfloat16)
    noisy_act = noisy_act.reshape(flat, horizon, action_dims)
    half_dim = w_time.shape[0] // 2
    frequencies = jnp.exp(
        -math.log(10000.0) * jnp.arange(half_dim, dtype=jnp.float32) / (half_dim - 1)
    )
    angles = tsteps.astype(jnp.float32)[:, :, None] * frequencies[None, None, :]
    embedded = jnp.concatenate([jnp.sin(angles), jnp.cos(angles)], axis=2)
    time_act = mish_value(embedded).astype(jnp.bfloat16).reshape(flat, 2 * half_dim)
    time_film = jnp.dot(time_act, w_time, preferred_element_type=jnp.float32)
    columns_in = columns(noisy_act).reshape(flat * horizon, -1)
    weights = jnp.broadcast_to(advantage.reshape(flat, 1), (flat, horizon))
    return (
        time_act,
        time_film,
        columns_in,
        noisy_act.reshape(flat * horizon, action_dims),
        noise.reshape(flat * horizon, action_dims),
        weights.reshape(flat * horizon, 1),
    )


def mish_both(values):
    small = jnp.exp(-jnp.abs(values))
    positive = values >= 0
    top = jnp.where(positive, 1.0 + 2.0 * small, small * (small + 2.0))
    bottom = top + jnp.where(positive, 2.0 * small * small, 2.0)
    inverse = 1.0 / (bottom * (1.0 + small))
    soft = top * (1.0 + small) * inverse
    sigmoid = jnp.where(positive, 1.0, small) * bottom * inverse
    return values * soft, soft + values * sigmoid * (1.0 - soft * soft)


def denoise_kernel(
    core_ref,
    film_ref,
    columns_ref,
    noisy_ref,
    noise_ref,
    weight_ref,
    time_ref,
    w_in_ref,
    w_mid_ref,
    w_res_ref,
    w_out_ref,
    kept_ref,
    sent_ref,
    film_grad_ref,
    first_ref,
    act_ref,
    slope_ref,
    second_ref,
    work_ref,
    taps_ref,
    grad_ref,
    mid_ref,
    packed_ref,
    sums_ref,
    more_ref,
    stat_ref,
    stats_ref,
    *,
    horizon,
):
    flat = film_ref.shape[0]
    channels = w_mid_ref.shape[1]
    action_dims = noise_ref.shape[1]
    group_size = channels // GROUPS
    count = group_size * horizon
    row_group = lax.broadcasted_iota(jnp.int32, (channels, channels), 0) // group_size
    lane_group = lax.broadcasted_iota(jnp.int32, (channels, channels), 1) // group_size
    same_group = (row_group == lane_group).astype(jnp.float32)
    step = lax.broadcasted_iota(jnp.int32, (horizon, channels), 0)

    def rows_of(f):
        return pl.ds(pl.multiple_of(f * horizon, horizon), horizon)

    def one(f):
        return pl.ds(f, 1)

    def group_mean(ref):
        return (
            jnp.dot(
                ref[...],
                same_group,
                precision=lax.Precision.HIGHEST,
                preferred_element_type=jnp.float32,
            )
            / count
        )

    def column_sum(values):
        return jnp.sum(values, axis=0, keepdims=True)

    def each(body):
        def run(f, carry):
            body(f)
            return carry

        lax.fori_loop(0, flat, run, 0)

    def shifted(values, distance):
        if distance == 0:
            return values
        rolled = pltpu.roll(values, (-distance) % horizon, 0)
        inside = jnp.logical_and(step + distance >= 0, step + distance < horizon)
        return jnp.where(inside, rolled, 0.0)

    def normalize(ref):
        def means(f):
            sums_ref[one(f), :] = column_sum(ref[rows_of(f), :])

        each(means)
        stat_ref[...] = group_mean(sums_ref)

        def squares(f):
            centred = ref[rows_of(f), :] - stat_ref[one(f), :]
            sums_ref[one(f), :] = column_sum(centred * centred)

        each(squares)
        stats_ref[...] = lax.rsqrt(group_mean(sums_ref) + 1e-05)

    first_ref[...] = jnp.dot(columns_ref[...], w_in_ref[...], preferred_element_type=jnp.float32)
    normalize(first_ref)
    first_inverse = stats_ref[...]

    def modulate(f):
        rows = rows_of(f)
        normed = (first_ref[rows, :] - stat_ref[one(f), :]) * stats_ref[one(f), :]
        act, slope = mish_both(normed)
        first_ref[rows, :] = normed
        act_ref[rows, :] = act
        slope_ref[rows, :] = slope
        modulated = film_ref[one(f), :channels] * act + film_ref[one(f), channels:]
        for tap in range(5):
            taps_ref[rows, tap * channels : (tap + 1) * channels] = shifted(
                modulated, tap - 2
            ).astype(jnp.bfloat16)

    each(modulate)

    second_ref[...] = jnp.dot(taps_ref[...], w_mid_ref[...], preferred_element_type=jnp.float32)
    normalize(second_ref)
    second_inverse = stats_ref[...]
    work_ref[...] = jnp.dot(noisy_ref[...], w_res_ref[...], preferred_element_type=jnp.float32)

    def activate(f):
        rows = rows_of(f)
        normed = (second_ref[rows, :] - stat_ref[one(f), :]) * stats_ref[one(f), :]
        act, slope = mish_both(normed)
        second_ref[rows, :] = normed
        grad_ref[rows, :] = (act + work_ref[rows, :]).astype(jnp.bfloat16)
        work_ref[rows, :] = slope

    each(activate)
    block_out = grad_ref[...]
    errors = jnp.dot(block_out, w_out_ref[...], preferred_element_type=jnp.float32)
    errors = errors - noise_ref[...].astype(jnp.float32)
    scale = 1.0 / (horizon * action_dims)
    err_sum = jnp.sum(jnp.sum(errors * errors, axis=1, keepdims=True), axis=0, keepdims=True)
    err_sum = err_sum * scale
    d_pred = (2.0 * weight_ref[...] * errors * scale).astype(jnp.bfloat16)
    over_rows = (((0,), (0,)), ((), ()))
    over_lanes = (((1,), (1,)), ((), ()))
    grad_out = lax.dot_general(
        d_pred, block_out, over_rows, preferred_element_type=jnp.float32
    )
    d_block = lax.dot_general(
        d_pred, w_out_ref[...], over_lanes, preferred_element_type=jnp.float32
    )
    grad_res = lax.dot_general(
        noisy_ref[...],
        d_block.astype(jnp.bfloat16),
        over_rows,
        preferred_element_type=jnp.float32,
    )
    work_ref[...] = work_ref[...] * d_block

    def back_sums(normed_ref):
        def sums(f):
            rows = rows_of(f)
            work = work_ref[rows, :]
            sums_ref[one(f), :] = column_sum(work)
            more_ref[one(f), :] = column_sum(work * normed_ref[rows, :])

        each(sums)

    def back(normed_ref, inverse):
        stat_ref[...] = group_mean(sums_ref) * inverse
        more_ref[...] = group_mean(more_ref) * inverse
        stats_ref[...] = inverse

        def apply(f):
            rows = rows_of(f)
            grad = work_ref[rows, :] * stats_ref[one(f), :] - stat_ref[one(f), :]
            grad = grad - normed_ref[rows, :] * more_ref[one(f), :]
            grad_ref[rows, :] = grad.astype(jnp.bfloat16)

        each(apply)

    back_sums(second_ref)
    back(second_ref, second_inverse)
    for tap in range(5):
        lanes = slice(tap * channels, (tap + 1) * channels)
        mid_ref[lanes, :] = lax.dot_general(
            taps_ref[:, lanes], grad_ref[...], over_rows, preferred_element_type=jnp.float32
        )

    for tap in range(5):
        second_ref[...] = lax.dot_general(
            grad_ref[...],
            w_mid_ref[tap * channels : (tap + 1) * channels, :],
            over_lanes,
            preferred_element_type=jnp.float32,
        )

        def add(f, tap=tap):
            rows = rows_of(f)
            piece = shifted(second_ref[rows, :], 2 - tap)
            if tap == 0:
                work_ref[rows, :] = piece
            else:
                work_ref[rows, :] = work_ref[rows, :] + piece

        each(add)

    def film_sums(f):
        rows = rows_of(f)
        grad = work_ref[rows, :]
        sums_ref[one(f), :] = column_sum(grad * act_ref[rows, :])
        more_ref[one(f), :] = column_sum(grad)
        work_ref[rows, :] = grad * film_ref[one(f), :channels] * slope_ref[rows, :]

    each(film_sums)
    d_film = jnp.concatenate([sums_ref[...], more_ref[...]], axis=1)
    samples = film_grad_ref.shape[0]
    film_grad_ref[...] = jnp.sum(d_film.reshape(samples, flat // samples, 2 * channels), axis=1)
    back_sums(first_ref)
    back(first_ref, first_inverse)
    grad_in = lax.dot_general(
        columns_ref[...], grad_ref[...], over_rows, preferred_element_type=jnp.float32
    )
    grad_time = lax.dot_general(
        time_ref[...],
        d_film.astype(jnp.bfloat16),
        over_rows,
        preferred_element_type=jnp.float32,
    )

    segments, groups, height, wide = kept_ref.shape
    lanes = wide // 2
    mid_rows, in_rows, side_rows, tall = layout_of(
        w_mid_ref.shape[0], w_in_ref.shape[0], w_res_ref.shape[0], time_ref.shape[1]
    )
    packed_ref[...] = jnp.zeros_like(packed_ref)
    err_row = jnp.broadcast_to(err_sum, (1, lanes))
    for s in range(segments):
        cols = slice(s * lanes, (s + 1) * lanes)
        packed_ref[s, :mid_rows, :] = jnp.concatenate(
            [mid_ref[:mid_rows, cols], mid_ref[mid_rows:, cols]], axis=1
        )
        packed_ref[s, mid_rows : mid_rows + w_in_ref.shape[0], :lanes] = grad_in[:, cols]
        packed_ref[s, mid_rows : mid_rows + action_dims, lanes:] = grad_res[:, cols]
        begin = mid_rows + side_rows
        packed_ref[s, begin : begin + action_dims, lanes:] = grad_out[:, cols]
        begin = begin + side_rows
        packed_ref[s, begin : begin + 1, lanes:] = err_row
        begin = mid_rows + in_rows
        packed_ref[s, begin:tall, :] = grad_time[:, s * wide : (s + 1) * wide]
    core = core_ref[0]
    for d in range(groups):
        mine = pl.ds(pl.multiple_of((2 * d + core) * height, 8), height)
        other = pl.ds(pl.multiple_of((2 * d + 1 - core) * height, 8), height)
        for s in range(segments):
            kept_ref[s, d] = packed_ref[s, mine, :]
            sent_ref[s, d] = packed_ref[s, other, :].astype(jnp.bfloat16)


def layout_of(mid, taps, action_dims, time):
    side_rows = -(-action_dims // 8) * 8
    in_rows = max(-(-taps // 8) * 8, 2 * side_rows + 8)
    return mid // 2, in_rows, side_rows, mid // 2 + in_rows + time


def trunk_kernel(order_ref, *refs, count, blocks, main, rest, fixed):
    row_refs, refs = refs[:count], refs[count:]
    gain_ref, refs = refs[0], refs[1:]
    gate_up_refs, refs = refs[: 2 * blocks], refs[2 * blocks :]
    down_refs, refs = refs[: 2 * blocks], refs[2 * blocks :]
    out_refs, refs = refs[:-5], refs[-5:]
    normed_ref, hidden_ref, gate_up_held, down_held, sems = refs
    loads = []
    for i, (source, held) in enumerate(
        [(ref, gate_up_held) for ref in gate_up_refs] + [(ref, down_held) for ref in down_refs]
    ):
        size = source.shape[0]
        place = held.at[pl.ds(i % (2 * blocks) * size, size)]
        loads.append(pltpu.make_async_copy(source, place, sems.at[i]))
    for load in loads:
        load.start()
    parts = normed_ref.shape[0]
    width = normed_ref.shape[2]
    size = parts // blocks

    def place_of(k):
        return k if fixed else order_ref[k]

    start = 0
    for row_ref in row_refs:
        rows = row_ref.shape[0]
        wide = row_ref[...].astype(jnp.float32)
        factor = lax.rsqrt(jnp.mean(wide * wide, axis=1, keepdims=True) + 1e-05)
        normed = (wide * factor * gain_ref[...]).astype(jnp.bfloat16)
        for j in range(parts):
            normed_ref[j, start : start + rows, :] = normed[:, j * width : (j + 1) * width]
        start += rows
    for i in range(2):
        both = 0.0
        for k in range(parts):
            if k % size == 0:
                loads[i * blocks + k // size].wait()
            both = both + jnp.dot(
                normed_ref[place_of(k)],
                gate_up_held[i * parts + k],
                preferred_element_type=jnp.float32,
            )
        if main:
            gate, up = both[:, :main], both[:, main : 2 * main]
            hidden_ref[i, :, :main] = (gate * jax.nn.sigmoid(gate) * up).astype(jnp.bfloat16)
        if rest:
            gate, up = both[:, 2 * main : 2 * main + rest], both[:, 2 * main + rest :]
            hidden_ref[i, :, main:] = (gate * jax.nn.sigmoid(gate) * up).astype(jnp.bfloat16)
    for k in range(parts):
        if k % size == 0:
            loads[2 * blocks + k // size].wait()
            loads[3 * blocks + k // size].wait()
        piece = jnp.dot(hidden_ref[0], down_held[k], preferred_element_type=jnp.float32)
        piece = piece + jnp.dot(
            hidden_ref[1], down_held[parts + k], preferred_element_type=jnp.float32
        )
        begin = place_of(k) * width
        if not fixed:
            begin = pl.multiple_of(begin, LANES)
        start = 0
        for out_ref in out_refs:
            rows = out_ref.shape[0]
            out_ref[:, pl.ds(begin, width)] = piece[start : start + rows].astype(out_ref.dtype)
            start += rows


def split_hidden(values, parts, dim):
    width = values.shape[dim] // parts
    main = width // LANES * LANES
    rest = width - main
    blocks = []
    for j in range(parts):
        first = lax.slice_in_dim(values, j * main, (j + 1) * main, axis=dim)
        begin = parts * main + j * rest
        last = lax.slice_in_dim(values, begin, begin + rest, axis=dim)
        blocks.append((first, last))
    return blocks, main, rest


def body(
    trunk_in,
    norm_gain,
    w_gate,
    w_up,
    w_down,
    w_cond,
    w_time,
    w_in,
    w_mid,
    w_res,
    w_out,
    tsteps,
    advantage,
    actions,
    noise,
):
    segments = lax.axis_size("segment")
    segment_index = lax.axis_index("segment")
    core_index = lax.axis_index("mp")
    groups = lax.axis_size("dp")
    group_index = lax.axis_index("dp")
    is_first = segment_index == 0
    is_last = segment_index == segments - 1

    half = trunk_in.shape[1]
    width = 2 * half
    gain = norm_gain.astype(jnp.float32)
    micro_count = segments * REPEAT
    rows = trunk_in.shape[0] // (2 * micro_count)

    def ordered(own, other, axis):
        return jnp.where(
            core_index == 0,
            jnp.concatenate([own, other], axis=axis),
            jnp.concatenate([other, own], axis=axis),
        )

    shares = trunk_in.reshape(micro_count, 2, rows, half)
    kept = lax.dynamic_index_in_dim(shares, core_index, 1, keepdims=False)
    traded = swap(lax.dynamic_index_in_dim(shares, 1 - core_index, 1, keepdims=False), "mp", 1)
    inputs = ordered(kept, traded, 2)

    early = [gather(inputs[k], "dp") for k in range(LAG)]
    w_cond_both = ordered(w_cond, swap(w_cond, "mp", 1), 0)

    local_samples = tsteps.shape[0]
    share = local_samples // segments
    own_rows = share // 2
    begin_row = segment_index * share + core_index * own_rows

    def own_part(values):
        return lax.dynamic_slice_in_dim(values, begin_row, own_rows, 0)

    prepared = prepare(
        own_part(tsteps), own_part(advantage), own_part(actions), own_part(noise), w_time
    )
    gates, main, rest = split_hidden(w_gate[0], groups, 1)
    ups, _, _ = split_hidden(w_up[0], groups, 1)
    gate_up = jnp.stack(
        [jnp.concatenate([g[0], u[0], g[1], u[1]], axis=1) for g, u in zip(gates, ups)]
    )
    downs, _, _ = split_hidden(w_down[0], groups, 0)
    down = jnp.stack([jnp.concatenate(d, axis=0) for d in downs])

    def traded_blocks(blocks):
        if few("dp"):
            got = []
            for k in range(groups):
                piece = lax.dynamic_slice_in_dim(blocks, group_index ^ k, 1, 0)
                got.append(swap(piece, "dp", k) if k else piece)
        else:
            got = [lax.all_to_all(blocks, "dp", 0, 0, tiled=True)]
        return got + [swap(piece, "mp", 1) for piece in got]

    gate_ups = traded_blocks(gate_up)
    downs = traded_blocks(down)
    order = (group_index ^ jnp.arange(groups)).astype(jnp.int32)
    order, w_cond_both, prepared = lax.optimization_barrier((order, w_cond_both, prepared))

    def layer(current, pieces):
        count = len(pieces)
        whole = pl.BlockSpec(memory_space=pltpu.VMEM)
        if few("dp"):
            shapes = [jax.ShapeDtypeStruct((rows, width), jnp.float32)]
            shapes += [jax.ShapeDtypeStruct((rows, width), jnp.bfloat16)] * (groups - 1)
        else:
            shapes = [jax.ShapeDtypeStruct((groups * rows, width), jnp.float32)]
        total = groups * rows
        partial = pl.pallas_call(
            functools.partial(
                trunk_kernel,
                count=count,
                blocks=len(gate_ups) // 2,
                main=main,
                rest=rest,
                fixed=not few("dp"),
            ),
            out_shape=shapes,
            in_specs=[pl.BlockSpec(memory_space=pltpu.SMEM)]
            + [whole] * (count + 1)
            + [pl.BlockSpec(memory_space=pl.ANY)] * (2 * len(gate_ups)),
            out_specs=[whole] * len(shapes),
            scratch_shapes=[
                pltpu.VMEM((groups, total, width // groups), jnp.bfloat16),
                pltpu.VMEM((2, total, main + rest), jnp.bfloat16),
                pltpu.VMEM((2 * groups,) + gate_up.shape[1:], jnp.bfloat16),
                pltpu.VMEM((2 * groups,) + down.shape[1:], jnp.bfloat16),
                pltpu.SemaphoreType.DMA((2 * len(gate_ups),)),
            ],
            compiler_params=pltpu.CompilerParams(vmem_limit_bytes=VMEM_LIMIT),
            name="trunk",
        )(order, *pieces, gain, *gate_ups, *downs)
        result = current.astype(jnp.float32)
        if few("dp"):
            result = result + partial[0]
            for k in range(1, groups):
                result = result + swap(partial[k], "dp", k).astype(jnp.float32)
        else:
            result = result + scatter_sum(partial[0], "dp", 0)
        return result.astype(jnp.bfloat16)

    passed = {}
    finished = []
    slots = micro_count + LAG * (segments - 1)
    for slot in range(slots):
        current = inputs[slot] if slot < micro_count else None
        received = passed.pop(slot - LAG, None)
        if current is None:
            current = received
        elif received is not None:
            current = jnp.where(is_first, current, received)
        result = layer(current, early[slot] if slot < LAG else gather(current, "dp"))
        if slot + LAG < slots and segments > 1:
            passed[slot] = hop(result, "segment")
        if slot >= LAG * (segments - 1):
            finished.append(result)

    tokens = trunk_in.shape[0] // local_samples
    conds = []
    for result in finished:
        averaged = jnp.mean(result.astype(jnp.float32).reshape(-1, tokens, width), axis=1)
        conds.append(averaged.astype(jnp.bfloat16))
    conds = [
        jnp.concatenate(conds[i * REPEAT : (i + 1) * REPEAT], axis=0) for i in range(segments)
    ]
    cond = jnp.where(is_last, conds[-1], jnp.zeros_like(conds[-1]))
    for i in range(segments - 1):
        cond = cond + lax.ppermute(conds[i], "segment", [(segments - 1, i)])
    cond_act = mish_value(cond.astype(jnp.float32)).astype(jnp.bfloat16)
    film_cond = jnp.dot(
        cond_act, w_cond_both, preferred_element_type=jnp.float32
    )
    cond_kept = lax.dynamic_slice_in_dim(cond, core_index * half, half, 1)
    cond_sent = lax.dynamic_slice_in_dim(cond, (1 - core_index) * half, half, 1)
    cond_wide = ordered(cond_kept, swap(cond_sent, "mp", 1), 0).astype(jnp.float32)
    act_half = mish_value(cond_wide).astype(jnp.bfloat16)
    time_act, time_film, columns_in, noisy, noise_rows, weights = prepared
    flat = time_act.shape[0]
    film = film_cond[:, None, :] + time_film.reshape(own_rows, -1, film_cond.shape[1])
    film = film.reshape(flat, -1)
    channels = w_mid.shape[1]
    lanes = channels // segments
    taps = w_in.shape[0]
    action_dims = w_res.shape[0]
    mid_rows, in_rows, side_rows, tall = layout_of(
        w_mid.shape[0], taps, action_dims, w_time.shape[0]
    )
    height = -(-tall // (16 * groups)) * 8
    rows_all = columns_in.shape[0]
    vmem = pl.BlockSpec(memory_space=pltpu.VMEM)
    block = (segments, groups, height, 2 * lanes)
    kept, traded, d_film_cond = pl.pallas_call(
        functools.partial(denoise_kernel, horizon=rows_all // flat),
        out_shape=(
            jax.ShapeDtypeStruct(block, jnp.float32),
            jax.ShapeDtypeStruct(block, jnp.bfloat16),
            jax.ShapeDtypeStruct((own_rows, 2 * channels), jnp.float32),
        ),
        in_specs=[pl.BlockSpec(memory_space=pltpu.SMEM)] + [vmem] * 10,
        out_specs=(vmem, vmem, vmem),
        scratch_shapes=[pltpu.VMEM((rows_all, channels), jnp.float32)] * 5
        + [
            pltpu.VMEM((rows_all, w_mid.shape[0]), jnp.bfloat16),
            pltpu.VMEM((rows_all, channels), jnp.bfloat16),
            pltpu.VMEM(w_mid.shape, jnp.float32),
            pltpu.VMEM((segments, 2 * groups * height, 2 * lanes), jnp.float32),
        ]
        + [pltpu.VMEM((flat, channels), jnp.float32)] * 4,
        compiler_params=pltpu.CompilerParams(vmem_limit_bytes=VMEM_LIMIT),
        name="denoise",
    )(
        core_index.astype(jnp.int32).reshape(1),
        film,
        columns_in,
        noisy,
        noise_rows,
        weights,
        time_act,
        w_in,
        w_mid,
        w_res,
        w_out,
    )
    film_own = d_film_cond.astype(jnp.bfloat16)
    film_all = ordered(film_own, swap(film_own, "mp", 1), 0)
    grad_cond = contract("sc,dc->sd", film_all, w_cond) * mish_slope(cond_wide)

    total = segments * groups
    part = (kept + swap(traded, "mp", 1).astype(jnp.float32)).astype(jnp.bfloat16)
    part = part.reshape(total, height, 2 * lanes)
    acts = jnp.broadcast_to(act_half.reshape(1, -1, 2 * lanes), (total, share * half // (2 * lanes), 2 * lanes))
    films = film_all.reshape(share, segments, 1, 2 * lanes).transpose(1, 2, 0, 3)
    films = jnp.broadcast_to(films, (segments, groups, share, 2 * lanes))
    films = films.reshape(total, share, 2 * lanes)
    got = lax.all_to_all(
        jnp.concatenate([part, acts, films], axis=1), ("segment", "dp"), 0, 0, tiled=True
    )
    split = height + acts.shape[1]
    part = jnp.sum(got[:, :height].astype(jnp.float32), axis=0).astype(jnp.bfloat16)
    summed = everywhere(part, ("dp", "mp"))
    acts = got[:, height:split].reshape(total * share, half)
    films = got[:, split:].reshape(total * share, 2 * lanes)
    grad_w_cond = contract("sd,sc->dc", acts, films)

    summed = summed.astype(jnp.float32)
    low, high = summed[:, :lanes], summed[:, lanes:]
    begin = mid_rows + 2 * side_rows
    loss = (high[begin, :1] / (groups * local_samples * tsteps.shape[1])).reshape(1)
    pieces = [
        jnp.concatenate([low[:mid_rows], high[:mid_rows]], axis=0),
        low[mid_rows : mid_rows + taps],
        high[mid_rows : mid_rows + action_dims],
        high[mid_rows + side_rows : mid_rows + side_rows + action_dims],
    ]
    grad_w_time = summed[mid_rows + in_rows : tall]
    return (
        pieces[1],
        pieces[0],
        pieces[2],
        pieces[3].T,
        grad_w_time,
        grad_w_cond,
        grad_cond,
        loss,
    )


def solution(mesh):
    in_specs = (
        P("dp", "mp"),
        P("segment", None),
        P("segment", "dp", "mp"),
        P("segment", "dp", "mp"),
        P("segment", "mp", "dp"),
        P("mp", None),
        P(),
        P(),
        P(),
        P(),
        P(),
        P("dp", None),
        P("dp", None),
        P("dp", None, None),
        P("dp", None, None, None),
    )
    out_specs = (
        P(None, "segment"),
        P(None, "segment"),
        P(None, "segment"),
        P("segment", None),
        P(None, "segment"),
        P("mp", "segment"),
        P(("dp", "segment"), "mp"),
        P(),
    )
    return jax.shard_map(body, mesh=mesh, in_specs=in_specs, out_specs=out_specs, check_vma=False)
```

```python
import functools
import math

import jax
import jax.numpy as jnp
from jax import lax
from jax.experimental import pallas as pl
from jax.experimental.pallas import tpu as pltpu
from jax.sharding import PartitionSpec as P

GROUPS = 8
TSTEPS = 100
LAG = 2
REPEAT = 1
DIRECT = 4
LANES = 128
VMEM_LIMIT = 24 * 2**20
TRUNK_VMEM = 16 * 2**20


def swap(value, axis, distance):
    size = lax.axis_size(axis)
    return lax.ppermute(value, axis, [(i, i ^ distance) for i in range(size)])


def hop(value, axis, odd):
    size = lax.axis_size(axis)
    got = []
    for start in (0, 1):
        pairs = [(i, i + 1) for i in range(start, size - 1, 2)]
        pairs += [(j, i) for i, j in pairs]
        got.append(lax.ppermute(value, axis, pairs) if pairs else value)
    return jnp.where(odd, got[0], got[1])


def few(axis):
    return lax.axis_size(axis) <= DIRECT


def gather(value, axis):
    if few(axis):
        return [value] + [swap(value, axis, k) for k in range(1, lax.axis_size(axis))]
    stacked = lax.all_gather(value, axis, axis=0, tiled=True)
    return [stacked]


def everywhere(value, axes):
    size = math.prod(lax.axis_size(axis) for axis in axes)
    sent = jnp.broadcast_to(value[None], (size,) + value.shape)
    got = lax.all_to_all(sent, axes, 0, 0, tiled=True)
    return got.reshape((-1,) + value.shape[1:])


def scatter_sum(value, axis, dim):
    size = lax.axis_size(axis)
    width = value.shape[dim] // size
    index = lax.axis_index(axis)
    if not few(axis):
        sent = jnp.stack(jnp.split(value.astype(jnp.bfloat16), size, axis=dim))
        got = lax.all_to_all(sent, axis, 0, 0, tiled=True)
        return jnp.sum(got.astype(jnp.float32), axis=0)
    total = lax.dynamic_slice_in_dim(value, index * width, width, dim)
    for k in range(1, size):
        piece = lax.dynamic_slice_in_dim(value, (index ^ k) * width, width, dim)
        total = total + swap(piece.astype(jnp.bfloat16), axis, k).astype(jnp.float32)
    return total


def mish_value(values):
    return values * jnp.tanh(jax.nn.softplus(values))


def mish_slope(values):
    soft = jnp.tanh(jax.nn.softplus(values))
    return soft + values * jax.nn.sigmoid(values) * (1.0 - soft * soft)


def contract(form, left, right):
    return jnp.einsum(form, left, right, preferred_element_type=jnp.float32)


def alpha_table():
    grid = jnp.arange(TSTEPS + 1, dtype=jnp.float32) / TSTEPS
    curve = jnp.cos((grid + 0.008) / 1.008 * math.pi / 2.0) ** 2
    betas = jnp.minimum(1.0 - curve[1:] / curve[:-1], 0.999)
    return jnp.cumprod(1.0 - betas)


def columns(values):
    steps = values.shape[1]
    padded = jnp.pad(values, ((0, 0), (2, 2), (0, 0)))
    return jnp.concatenate([padded[:, tap : tap + steps] for tap in range(5)], axis=2)


def prepare(tsteps, advantage, actions, noise, w_time):
    row_count, levels = tsteps.shape
    horizon, action_dims = (actions.shape[1], actions.shape[2])
    flat = row_count * levels
    matches = (tsteps[:, :, None] == jnp.arange(TSTEPS, dtype=jnp.int32)[None, None, :]).astype(
        jnp.float32
    )
    alpha = jnp.sum(matches * alpha_table()[None, None, :], axis=2)
    keep_root = jnp.sqrt(alpha)[:, :, None, None]
    noise_root = jnp.sqrt(1.0 - alpha)[:, :, None, None]
    noisy_act = (
        keep_root * actions.astype(jnp.float32)[:, None] + noise_root * noise.astype(jnp.float32)
    ).astype(jnp.bfloat16)
    noisy_act = noisy_act.reshape(flat, horizon, action_dims)
    half_dim = w_time.shape[0] // 2
    frequencies = jnp.exp(
        -math.log(10000.0) * jnp.arange(half_dim, dtype=jnp.float32) / (half_dim - 1)
    )
    angles = tsteps.astype(jnp.float32)[:, :, None] * frequencies[None, None, :]
    embedded = jnp.concatenate([jnp.sin(angles), jnp.cos(angles)], axis=2)
    time_act = mish_value(embedded).astype(jnp.bfloat16).reshape(flat, 2 * half_dim)
    time_film = jnp.dot(time_act, w_time, preferred_element_type=jnp.float32)
    columns_in = columns(noisy_act).reshape(flat * horizon, -1)
    return (
        time_act,
        time_film,
        columns_in,
        noisy_act.reshape(flat * horizon, action_dims),
        noise.reshape(flat * horizon, action_dims),
        jnp.broadcast_to(advantage.reshape(flat, 1, 1), (flat, horizon, action_dims)).reshape(
            flat * horizon, action_dims
        ),
    )


def mish_both(values):
    small = jnp.exp(-jnp.abs(values))
    positive = values >= 0
    top = jnp.where(positive, 1.0 + 2.0 * small, small * (small + 2.0))
    bottom = top + jnp.where(positive, 2.0 * small * small, 2.0)
    inverse = 1.0 / (bottom * (1.0 + small))
    soft = top * (1.0 + small) * inverse
    sigmoid = jnp.where(positive, 1.0, small) * bottom * inverse
    return values * soft, soft + values * sigmoid * (1.0 - soft * soft)


def denoise_kernel(
    core_ref,
    film_ref,
    columns_ref,
    noisy_ref,
    noise_ref,
    weight_ref,
    time_ref,
    w_in_ref,
    w_mid_ref,
    w_res_ref,
    w_out_ref,
    kept_ref,
    sent_ref,
    film_grad_ref,
    first_ref,
    act_ref,
    slope_ref,
    second_ref,
    work_ref,
    taps_ref,
    grad_ref,
    mid_ref,
    packed_ref,
    sums_ref,
    more_ref,
    stat_ref,
    stats_ref,
    *,
    horizon,
):
    flat = film_ref.shape[0]
    channels = w_mid_ref.shape[1]
    action_dims = noise_ref.shape[1]
    group_size = channels // GROUPS
    count = group_size * horizon
    row_group = lax.broadcasted_iota(jnp.int32, (channels, channels), 0) // group_size
    lane_group = lax.broadcasted_iota(jnp.int32, (channels, channels), 1) // group_size
    same_group = (row_group == lane_group).astype(jnp.float32)
    step = lax.broadcasted_iota(jnp.int32, (horizon, channels), 0)

    def rows_of(f):
        return pl.ds(pl.multiple_of(f * horizon, horizon), horizon)

    def one(f):
        return pl.ds(f, 1)

    def group_mean(ref):
        return (
            jnp.dot(
                ref[...],
                same_group,
                precision=lax.Precision.HIGHEST,
                preferred_element_type=jnp.float32,
            )
            / count
        )

    def column_sum(values):
        return jnp.sum(values, axis=0, keepdims=True)

    def each(body):
        def run(f, carry):
            body(f)
            return carry

        lax.fori_loop(0, flat, run, 0)

    def shifted(values, distance):
        if distance == 0:
            return values
        rolled = pltpu.roll(values, (-distance) % horizon, 0)
        inside = jnp.logical_and(step + distance >= 0, step + distance < horizon)
        return jnp.where(inside, rolled, 0.0)

    def normalize(ref):
        def means(f):
            sums_ref[one(f), :] = column_sum(ref[rows_of(f), :])

        each(means)
        stat_ref[...] = group_mean(sums_ref)

        def squares(f):
            centred = ref[rows_of(f), :] - stat_ref[one(f), :]
            sums_ref[one(f), :] = column_sum(centred * centred)

        each(squares)
        stats_ref[...] = lax.rsqrt(group_mean(sums_ref) + 1e-05)

    first_ref[...] = jnp.dot(columns_ref[...], w_in_ref[...], preferred_element_type=jnp.float32)
    normalize(first_ref)
    first_inverse = stats_ref[...]

    def modulate(f):
        rows = rows_of(f)
        normed = (first_ref[rows, :] - stat_ref[one(f), :]) * stats_ref[one(f), :]
        act, slope = mish_both(normed)
        first_ref[rows, :] = normed
        act_ref[rows, :] = act
        slope_ref[rows, :] = slope
        modulated = film_ref[one(f), :channels] * act + film_ref[one(f), channels:]
        for tap in range(5):
            taps_ref[rows, tap * channels : (tap + 1) * channels] = shifted(
                modulated, tap - 2
            ).astype(jnp.bfloat16)

    each(modulate)

    second_ref[...] = jnp.dot(taps_ref[...], w_mid_ref[...], preferred_element_type=jnp.float32)
    normalize(second_ref)
    second_inverse = stats_ref[...]
    work_ref[...] = jnp.dot(noisy_ref[...], w_res_ref[...], preferred_element_type=jnp.float32)

    def activate(f):
        rows = rows_of(f)
        normed = (second_ref[rows, :] - stat_ref[one(f), :]) * stats_ref[one(f), :]
        act, slope = mish_both(normed)
        second_ref[rows, :] = normed
        grad_ref[rows, :] = (act + work_ref[rows, :]).astype(jnp.bfloat16)
        work_ref[rows, :] = slope

    each(activate)
    block_out = grad_ref[...]
    over_rows = (((0,), (0,)), ((), ()))
    over_lanes = (((1,), (1,)), ((), ()))
    errors = lax.dot_general(
        block_out, w_out_ref[...], over_lanes, preferred_element_type=jnp.float32
    )
    errors = errors - noise_ref[...].astype(jnp.float32)
    scale = 1.0 / (horizon * action_dims)
    err_sum = jnp.sum(jnp.sum(errors * errors, axis=1, keepdims=True), axis=0, keepdims=True)
    err_sum = err_sum * scale
    d_pred = (2.0 * weight_ref[...] * errors * scale).astype(jnp.bfloat16)
    grad_out = lax.dot_general(
        d_pred, block_out, over_rows, preferred_element_type=jnp.float32
    )
    d_block = jnp.dot(d_pred, w_out_ref[...], preferred_element_type=jnp.float32)
    grad_res = lax.dot_general(
        noisy_ref[...],
        d_block.astype(jnp.bfloat16),
        over_rows,
        preferred_element_type=jnp.float32,
    )
    work_ref[...] = work_ref[...] * d_block

    def back_sums(normed_ref):
        def sums(f):
            rows = rows_of(f)
            work = work_ref[rows, :]
            sums_ref[one(f), :] = column_sum(work)
            more_ref[one(f), :] = column_sum(work * normed_ref[rows, :])

        each(sums)

    def back(normed_ref, inverse):
        stat_ref[...] = group_mean(sums_ref) * inverse
        more_ref[...] = group_mean(more_ref) * inverse
        stats_ref[...] = inverse

        def apply(f):
            rows = rows_of(f)
            grad = work_ref[rows, :] * stats_ref[one(f), :] - stat_ref[one(f), :]
            grad = grad - normed_ref[rows, :] * more_ref[one(f), :]
            grad_ref[rows, :] = grad.astype(jnp.bfloat16)

        each(apply)

    back_sums(second_ref)
    back(second_ref, second_inverse)
    for tap in range(5):
        lanes = slice(tap * channels, (tap + 1) * channels)
        mid_ref[lanes, :] = lax.dot_general(
            taps_ref[:, lanes], grad_ref[...], over_rows, preferred_element_type=jnp.float32
        )

    for tap in range(5):
        second_ref[...] = lax.dot_general(
            grad_ref[...],
            w_mid_ref[tap * channels : (tap + 1) * channels, :],
            over_lanes,
            preferred_element_type=jnp.float32,
        )

        def add(f, tap=tap):
            rows = rows_of(f)
            piece = shifted(second_ref[rows, :], 2 - tap)
            if tap == 0:
                work_ref[rows, :] = piece
            else:
                work_ref[rows, :] = work_ref[rows, :] + piece

        each(add)

    def film_sums(f):
        rows = rows_of(f)
        grad = work_ref[rows, :]
        sums_ref[one(f), :] = column_sum(grad * act_ref[rows, :])
        more_ref[one(f), :] = column_sum(grad)
        work_ref[rows, :] = grad * film_ref[one(f), :channels] * slope_ref[rows, :]

    each(film_sums)
    d_film = jnp.concatenate([sums_ref[...], more_ref[...]], axis=1)
    samples = film_grad_ref.shape[0]
    film_grad_ref[...] = jnp.sum(d_film.reshape(samples, flat // samples, 2 * channels), axis=1)
    back_sums(first_ref)
    back(first_ref, first_inverse)
    grad_in = lax.dot_general(
        columns_ref[...], grad_ref[...], over_rows, preferred_element_type=jnp.float32
    )
    grad_time = lax.dot_general(
        time_ref[...],
        d_film.astype(jnp.bfloat16),
        over_rows,
        preferred_element_type=jnp.float32,
    )

    segments, groups, height, wide = kept_ref.shape
    lanes = wide // 2
    mid_rows, in_rows, side_rows, tall = layout_of(
        w_mid_ref.shape[0], w_in_ref.shape[0], w_res_ref.shape[0], time_ref.shape[1]
    )
    packed_ref[...] = jnp.zeros_like(packed_ref)
    err_row = jnp.broadcast_to(err_sum, (1, lanes))
    for s in range(segments):
        cols = slice(s * lanes, (s + 1) * lanes)
        packed_ref[s, :mid_rows, :] = jnp.concatenate(
            [mid_ref[:mid_rows, cols], mid_ref[mid_rows:, cols]], axis=1
        )
        packed_ref[s, mid_rows : mid_rows + w_in_ref.shape[0], :lanes] = grad_in[:, cols]
        packed_ref[s, mid_rows : mid_rows + action_dims, lanes:] = grad_res[:, cols]
        begin = mid_rows + side_rows
        packed_ref[s, begin : begin + action_dims, lanes:] = grad_out[:, cols]
        begin = begin + side_rows
        packed_ref[s, begin : begin + 1, lanes:] = err_row
        begin = mid_rows + in_rows
        packed_ref[s, begin:tall, :] = grad_time[:, s * wide : (s + 1) * wide]
    core = core_ref[0]
    for d in range(groups):
        mine = pl.ds(pl.multiple_of((2 * d + core) * height, 8), height)
        other = pl.ds(pl.multiple_of((2 * d + 1 - core) * height, 8), height)
        for s in range(segments):
            kept_ref[s, d] = packed_ref[s, mine, :]
            sent_ref[s, d] = packed_ref[s, other, :].astype(jnp.bfloat16)


def layout_of(mid, taps, action_dims, time):
    side_rows = -(-action_dims // 8) * 8
    in_rows = max(-(-taps // 8) * 8, 2 * side_rows + 8)
    return mid // 2, in_rows, side_rows, mid // 2 + in_rows + time


def load_kernel(*refs, blocks):
    sources, (gate_up_ref, down_ref, sems) = refs[: 4 * blocks], refs[4 * blocks :]
    loads = []
    for i, source in enumerate(sources):
        held = gate_up_ref if i < 2 * blocks else down_ref
        size = source.shape[0]
        place = held.at[pl.ds(i % (2 * blocks) * size, size)]
        loads.append(pltpu.make_async_copy(source, place, sems.at[i]))
    for load in loads:
        load.start()
    for load in loads:
        load.wait()


def trunk_kernel(order_ref, *refs, count, main, rest, fixed):
    row_refs, refs = refs[:count], refs[count:]
    gain_ref, gate_up_ref, down_ref = refs[:3]
    out_refs, (normed_ref, hidden_ref) = refs[3:-4], refs[-2:]
    parts, _, width = normed_ref.shape

    def place_of(k):
        return k if fixed else order_ref[k]

    start = 0
    for row_ref in row_refs:
        rows = row_ref.shape[0]
        wide = row_ref[...].astype(jnp.float32)
        factor = lax.rsqrt(jnp.mean(wide * wide, axis=1, keepdims=True) + 1e-05)
        normed = (wide * factor * gain_ref[...]).astype(jnp.bfloat16)
        for j in range(parts):
            normed_ref[j, start : start + rows, :] = normed[:, j * width : (j + 1) * width]
        start += rows

    def hide(i, carry):
        both = 0.0
        for k in range(parts):
            both = both + jnp.dot(
                normed_ref[place_of(k)],
                gate_up_ref[i * parts + k],
                preferred_element_type=jnp.float32,
            )
        if main:
            gate, up = both[:, :main], both[:, main : 2 * main]
            hidden_ref[i, :, :main] = (gate * jax.nn.sigmoid(gate) * up).astype(jnp.bfloat16)
        if rest:
            gate, up = both[:, 2 * main : 2 * main + rest], both[:, 2 * main + rest :]
            hidden_ref[i, :, main:] = (gate * jax.nn.sigmoid(gate) * up).astype(jnp.bfloat16)
        return carry

    lax.fori_loop(0, 2, hide, 0)

    def project(k, carry):
        piece = jnp.dot(hidden_ref[0], down_ref[k], preferred_element_type=jnp.float32)
        piece = piece + jnp.dot(
            hidden_ref[1], down_ref[parts + k], preferred_element_type=jnp.float32
        )
        begin = place_of(k) * width
        if not fixed:
            begin = pl.multiple_of(begin, LANES)
        start = 0
        for out_ref in out_refs:
            rows = out_ref.shape[0]
            out_ref[:, pl.ds(begin, width)] = piece[start : start + rows].astype(out_ref.dtype)
            start += rows
        return carry

    if fixed:
        for k in range(parts):
            project(k, 0)
    else:
        lax.fori_loop(0, parts, project, 0)


def split_hidden(values, parts, dim):
    width = values.shape[dim] // parts
    main = width // LANES * LANES
    rest = width - main
    blocks = []
    for j in range(parts):
        first = lax.slice_in_dim(values, j * main, (j + 1) * main, axis=dim)
        begin = parts * main + j * rest
        last = lax.slice_in_dim(values, begin, begin + rest, axis=dim)
        blocks.append((first, last))
    return blocks, main, rest


def body(
    trunk_in,
    norm_gain,
    w_gate,
    w_up,
    w_down,
    w_cond,
    w_time,
    w_in,
    w_mid,
    w_res,
    w_out,
    tsteps,
    advantage,
    actions,
    noise,
):
    segments = lax.axis_size("segment")
    segment_index = lax.axis_index("segment")
    core_index = lax.axis_index("mp")
    groups = lax.axis_size("dp")
    group_index = lax.axis_index("dp")
    is_first = segment_index == 0
    is_last = segment_index == segments - 1
    is_odd = segment_index % 2 == 1
    is_core = core_index == 1

    half = trunk_in.shape[1]
    width = 2 * half
    gain = norm_gain.astype(jnp.float32)
    micro_count = segments * REPEAT
    rows = trunk_in.shape[0] // (2 * micro_count)

    def ordered(own, other, axis):
        return jnp.where(
            is_core,
            jnp.concatenate([other, own], axis=axis),
            jnp.concatenate([own, other], axis=axis),
        )

    shares = trunk_in.reshape(micro_count, 2, rows, half)
    kept = lax.dynamic_index_in_dim(shares, core_index, 1, keepdims=False)
    traded = swap(lax.dynamic_index_in_dim(shares, 1 - core_index, 1, keepdims=False), "mp", 1)
    inputs = ordered(kept, traded, 2)

    local_samples = tsteps.shape[0]
    share = local_samples // segments
    own_rows = share // 2
    begin_row = segment_index * share + core_index * own_rows

    def own_part(values):
        return lax.dynamic_slice_in_dim(values, begin_row, own_rows, 0)

    gates, main, rest = split_hidden(w_gate[0], groups, 1)
    ups, _, _ = split_hidden(w_up[0], groups, 1)
    gate_up = jnp.stack(
        [jnp.concatenate([g[0], u[0], g[1], u[1]], axis=1) for g, u in zip(gates, ups)]
    )
    downs, _, _ = split_hidden(w_down[0], groups, 0)
    down = jnp.stack([jnp.concatenate(d, axis=0) for d in downs])

    def block(blocks, k):
        return lax.dynamic_slice_in_dim(blocks, group_index ^ k, 1, 0)

    near = [k for k in range(1, groups) if k & (k - 1) == 0]
    far = [k for k in range(1, groups) if k not in near]
    later = (inputs, w_cond, own_part(tsteps), own_part(advantage), own_part(actions), own_part(noise))
    if few("dp"):
        blocks = [[block(gate_up, k), block(down, k)] for k in range(groups)]
        blocks, later = lax.optimization_barrier((blocks, later))
        got = {0: blocks[0]}
        for k in near:
            got[k] = [swap(piece, "dp", k) for piece in blocks[k]]
    early = [gather(later[0][k], "dp") for k in range(LAG)]
    inputs = later[0]
    w_cond_other = swap(later[1], "mp", 1)
    prepared = prepare(*later[2:], w_time)
    if few("dp"):
        for k in far:
            got[k] = [swap(piece, "dp", k) for piece in blocks[k]]
        gate_ups = [got[k][0] for k in range(groups)]
        downs = [got[k][1] for k in range(groups)]
    else:
        gate_ups = [lax.all_to_all(gate_up, "dp", 0, 0, tiled=True)]
        downs = [lax.all_to_all(down, "dp", 0, 0, tiled=True)]
    gate_ups = gate_ups + [swap(piece, "mp", 1) for piece in gate_ups]
    downs = downs + [swap(piece, "mp", 1) for piece in downs]
    order = (group_index ^ jnp.arange(groups)).astype(jnp.int32)
    vmem = pl.BlockSpec(memory_space=pltpu.VMEM)
    gate_up_held, down_held = pl.pallas_call(
        functools.partial(load_kernel, blocks=len(gate_ups) // 2),
        out_shape=(
            pltpu.VMEM((2 * groups,) + gate_up.shape[1:], jnp.bfloat16),
            pltpu.VMEM((2 * groups,) + down.shape[1:], jnp.bfloat16),
        ),
        in_specs=[pl.BlockSpec(memory_space=pl.ANY)] * (2 * len(gate_ups)),
        out_specs=(vmem, vmem),
        scratch_shapes=[pltpu.SemaphoreType.DMA((2 * len(gate_ups),))],
        compiler_params=pltpu.CompilerParams(vmem_limit_bytes=TRUNK_VMEM),
        name="load",
    )(*gate_ups, *downs)
    order, w_cond_other, prepared, is_odd, is_first, is_last, is_core = lax.optimization_barrier(
        (order, w_cond_other, prepared, is_odd, is_first, is_last, is_core)
    )

    def layer(current, pieces, held):
        count = len(pieces)
        whole = pl.BlockSpec(memory_space=pltpu.VMEM)
        if few("dp"):
            shapes = [jax.ShapeDtypeStruct((rows, width), jnp.float32)]
            shapes += [jax.ShapeDtypeStruct((rows, width), jnp.bfloat16)] * (groups - 1)
        else:
            shapes = [jax.ShapeDtypeStruct((groups * rows, width), jnp.float32)]
        total = groups * rows
        shapes += [pltpu.VMEM(value.shape, value.dtype) for value in held]
        partial = pl.pallas_call(
            functools.partial(
                trunk_kernel, count=count, main=main, rest=rest, fixed=not few("dp")
            ),
            out_shape=shapes,
            in_specs=[pl.BlockSpec(memory_space=pltpu.SMEM)] + [whole] * (count + 3),
            out_specs=[whole] * len(shapes),
            scratch_shapes=[
                pltpu.VMEM((groups, total, width // groups), jnp.bfloat16),
                pltpu.VMEM((2, total, main + rest), jnp.bfloat16),
            ],
            compiler_params=pltpu.CompilerParams(vmem_limit_bytes=TRUNK_VMEM),
            input_output_aliases={count + 2: len(shapes) - 2, count + 3: len(shapes) - 1},
            name="trunk",
        )(order, *pieces, gain, *held)
        result = current.astype(jnp.float32)
        if few("dp"):
            result = result + partial[0]
            for k in range(1, groups):
                result = result + swap(partial[k], "dp", k).astype(jnp.float32)
        else:
            result = result + scatter_sum(partial[0], "dp", 0)
        return result.astype(jnp.bfloat16), partial[-2:]

    held = (gate_up_held, down_held)
    passed = {}
    finished = []
    slots = micro_count + LAG * (segments - 1)
    for slot in range(slots):
        current = inputs[slot] if slot < micro_count else None
        received = passed.pop(slot - LAG, None)
        if current is None:
            current = received
        elif received is not None:
            current = jnp.where(is_first, current, received)
        pieces = early[slot] if slot < LAG else gather(current, "dp")
        result, held = layer(current, pieces, held)
        if slot + LAG < slots and segments > 1:
            passed[slot] = hop(result, "segment", is_odd)
        if slot >= LAG * (segments - 1):
            finished.append(result)

    tokens = trunk_in.shape[0] // local_samples
    conds = []
    for result in finished:
        averaged = jnp.mean(result.astype(jnp.float32).reshape(-1, tokens, width), axis=1)
        conds.append(averaged.astype(jnp.bfloat16))
    conds = [
        jnp.concatenate(conds[i * REPEAT : (i + 1) * REPEAT], axis=0) for i in range(segments)
    ]
    cond = jnp.where(is_last, conds[-1], jnp.zeros_like(conds[-1]))
    for i in range(segments - 1):
        cond = cond + lax.ppermute(conds[i], "segment", [(segments - 1, i)])
    cond_act = mish_value(cond.astype(jnp.float32)).astype(jnp.bfloat16)
    act_kept = jnp.where(is_core, cond_act[:, half:], cond_act[:, :half])
    act_sent = jnp.where(is_core, cond_act[:, :half], cond_act[:, half:])
    film_cond = jnp.dot(act_kept, w_cond, preferred_element_type=jnp.float32)
    film_cond = film_cond + jnp.dot(act_sent, w_cond_other, preferred_element_type=jnp.float32)
    cond_kept = jnp.where(is_core, cond[:, half:], cond[:, :half])
    cond_sent = jnp.where(is_core, cond[:, :half], cond[:, half:])
    cond_wide = ordered(cond_kept, swap(cond_sent, "mp", 1), 0).astype(jnp.float32)
    act_half = mish_value(cond_wide).astype(jnp.bfloat16)
    time_act, time_film, columns_in, noisy, noise_rows, weights = prepared
    flat = time_act.shape[0]
    film = film_cond[:, None, :] + time_film.reshape(own_rows, -1, film_cond.shape[1])
    film = film.reshape(flat, -1)
    channels = w_mid.shape[1]
    lanes = channels // segments
    taps = w_in.shape[0]
    action_dims = w_res.shape[0]
    mid_rows, in_rows, side_rows, tall = layout_of(
        w_mid.shape[0], taps, action_dims, w_time.shape[0]
    )
    height = -(-tall // (16 * groups)) * 8
    rows_all = columns_in.shape[0]
    vmem = pl.BlockSpec(memory_space=pltpu.VMEM)
    block = (segments, groups, height, 2 * lanes)
    kept, traded, d_film_cond = pl.pallas_call(
        functools.partial(denoise_kernel, horizon=rows_all // flat),
        out_shape=(
            jax.ShapeDtypeStruct(block, jnp.float32),
            jax.ShapeDtypeStruct(block, jnp.bfloat16),
            jax.ShapeDtypeStruct((own_rows, 2 * channels), jnp.float32),
        ),
        in_specs=[pl.BlockSpec(memory_space=pltpu.SMEM)] + [vmem] * 10,
        out_specs=(vmem, vmem, vmem),
        scratch_shapes=[pltpu.VMEM((rows_all, channels), jnp.float32)] * 5
        + [
            pltpu.VMEM((rows_all, w_mid.shape[0]), jnp.bfloat16),
            pltpu.VMEM((rows_all, channels), jnp.bfloat16),
            pltpu.VMEM(w_mid.shape, jnp.float32),
            pltpu.VMEM((segments, 2 * groups * height, 2 * lanes), jnp.float32),
        ]
        + [pltpu.VMEM((flat, channels), jnp.float32)] * 4,
        compiler_params=pltpu.CompilerParams(vmem_limit_bytes=VMEM_LIMIT),
        name="denoise",
    )(
        core_index.astype(jnp.int32).reshape(1),
        film,
        columns_in,
        noisy,
        noise_rows,
        weights,
        time_act,
        w_in,
        w_mid,
        w_res,
        w_out.T,
    )
    film_own = d_film_cond.astype(jnp.bfloat16)
    film_all = ordered(film_own, swap(film_own, "mp", 1), 0)
    grad_cond = contract("sc,dc->sd", film_all, w_cond) * mish_slope(cond_wide)

    total = segments * groups
    part = (kept + swap(traded, "mp", 1).astype(jnp.float32)).astype(jnp.bfloat16)
    part = part.reshape(total, height, 2 * lanes)
    acts = jnp.broadcast_to(act_half.reshape(1, -1, 2 * lanes), (total, share * half // (2 * lanes), 2 * lanes))
    films = film_all.reshape(share, segments, 1, 2 * lanes).transpose(1, 2, 0, 3)
    films = jnp.broadcast_to(films, (segments, groups, share, 2 * lanes))
    films = films.reshape(total, share, 2 * lanes)
    got = lax.all_to_all(
        jnp.concatenate([part, acts, films], axis=1), ("segment", "dp"), 0, 0, tiled=True
    )
    split = height + acts.shape[1]
    part = jnp.sum(got[:, :height].astype(jnp.float32), axis=0).astype(jnp.bfloat16)
    summed = everywhere(part, ("dp", "mp"))
    acts = got[:, height:split].reshape(total * share, half)
    films = got[:, split:].reshape(total * share, 2 * lanes)
    grad_w_cond = contract("sd,sc->dc", acts, films)

    summed = summed.astype(jnp.float32)
    low, high = summed[:, :lanes], summed[:, lanes:]
    begin = mid_rows + 2 * side_rows
    loss = (high[begin, :1] / (groups * local_samples * tsteps.shape[1])).reshape(1)
    pieces = [
        jnp.concatenate([low[:mid_rows], high[:mid_rows]], axis=0),
        low[mid_rows : mid_rows + taps],
        high[mid_rows : mid_rows + action_dims],
        high[mid_rows + side_rows : mid_rows + side_rows + action_dims],
    ]
    grad_w_time = summed[mid_rows + in_rows : tall]
    return (
        pieces[1],
        pieces[0],
        pieces[2],
        pieces[3].T,
        grad_w_time,
        grad_w_cond,
        grad_cond,
        loss,
    )


def solution(mesh):
    in_specs = (
        P("dp", "mp"),
        P("segment", None),
        P("segment", "dp", "mp"),
        P("segment", "dp", "mp"),
        P("segment", "mp", "dp"),
        P("mp", None),
        P(),
        P(),
        P(),
        P(),
        P(),
        P("dp", None),
        P("dp", None),
        P("dp", None, None),
        P("dp", None, None, None),
    )
    out_specs = (
        P(None, "segment"),
        P(None, "segment"),
        P(None, "segment"),
        P("segment", None),
        P(None, "segment"),
        P("mp", "segment"),
        P(("dp", "segment"), "mp"),
        P(),
    )

    return jax.shard_map(body, mesh=mesh, in_specs=in_specs, out_specs=out_specs, check_vma=False)
```

```python
import functools
import math

import jax
import jax.numpy as jnp
from jax import lax
from jax.experimental import pallas as pl
from jax.experimental.pallas import tpu as pltpu
from jax.sharding import PartitionSpec as P

GROUPS = 8
TSTEPS = 100
LAG = 2
REPEAT = 1
DIRECT = 4
LANES = 128
VMEM_LIMIT = 24 * 2**20
TRUNK_VMEM = 16 * 2**20


def swap(value, axis, distance):
    size = lax.axis_size(axis)
    return lax.ppermute(value, axis, [(i, i ^ distance) for i in range(size)])


def hop(value, axis, odd):
    size = lax.axis_size(axis)
    got = []
    for start in (0, 1):
        pairs = [(i, i + 1) for i in range(start, size - 1, 2)]
        pairs += [(j, i) for i, j in pairs]
        got.append(lax.ppermute(value, axis, pairs) if pairs else value)
    return jnp.where(odd, got[0], got[1])


def few(axis):
    return lax.axis_size(axis) <= DIRECT


def gather(value, axis):
    if few(axis):
        return [value] + [swap(value, axis, k) for k in range(1, lax.axis_size(axis))]
    stacked = lax.all_gather(value, axis, axis=0, tiled=True)
    return [stacked]


def everywhere(value, axes):
    size = math.prod(lax.axis_size(axis) for axis in axes)
    sent = jnp.broadcast_to(value[None], (size,) + value.shape)
    got = lax.all_to_all(sent, axes, 0, 0, tiled=True)
    return got.reshape((-1,) + value.shape[1:])


def scatter_sum(value, axis, dim):
    size = lax.axis_size(axis)
    width = value.shape[dim] // size
    index = lax.axis_index(axis)
    if not few(axis):
        sent = jnp.stack(jnp.split(value.astype(jnp.bfloat16), size, axis=dim))
        got = lax.all_to_all(sent, axis, 0, 0, tiled=True)
        return jnp.sum(got.astype(jnp.float32), axis=0)
    total = lax.dynamic_slice_in_dim(value, index * width, width, dim)
    for k in range(1, size):
        piece = lax.dynamic_slice_in_dim(value, (index ^ k) * width, width, dim)
        total = total + swap(piece.astype(jnp.bfloat16), axis, k).astype(jnp.float32)
    return total


def mish_value(values):
    return values * jnp.tanh(jax.nn.softplus(values))


def mish_slope(values):
    soft = jnp.tanh(jax.nn.softplus(values))
    return soft + values * jax.nn.sigmoid(values) * (1.0 - soft * soft)


def contract(form, left, right):
    return jnp.einsum(form, left, right, preferred_element_type=jnp.float32)


def alpha_table():
    grid = jnp.arange(TSTEPS + 1, dtype=jnp.float32) / TSTEPS
    curve = jnp.cos((grid + 0.008) / 1.008 * math.pi / 2.0) ** 2
    betas = jnp.minimum(1.0 - curve[1:] / curve[:-1], 0.999)
    return jnp.cumprod(1.0 - betas)


def columns(values):
    steps = values.shape[1]
    padded = jnp.pad(values, ((0, 0), (2, 2), (0, 0)))
    return jnp.concatenate([padded[:, tap : tap + steps] for tap in range(5)], axis=2)


def prepare(tsteps, advantage, actions, noise, w_time):
    row_count, levels = tsteps.shape
    horizon, action_dims = (actions.shape[1], actions.shape[2])
    flat = row_count * levels
    matches = (tsteps[:, :, None] == jnp.arange(TSTEPS, dtype=jnp.int32)[None, None, :]).astype(
        jnp.float32
    )
    alpha = jnp.sum(matches * alpha_table()[None, None, :], axis=2)
    keep_root = jnp.sqrt(alpha)[:, :, None, None]
    noise_root = jnp.sqrt(1.0 - alpha)[:, :, None, None]
    noisy_act = (
        keep_root * actions.astype(jnp.float32)[:, None] + noise_root * noise.astype(jnp.float32)
    ).astype(jnp.bfloat16)
    noisy_act = noisy_act.reshape(flat, horizon, action_dims)
    half_dim = w_time.shape[0] // 2
    frequencies = jnp.exp(
        -math.log(10000.0) * jnp.arange(half_dim, dtype=jnp.float32) / (half_dim - 1)
    )
    angles = tsteps.astype(jnp.float32)[:, :, None] * frequencies[None, None, :]
    embedded = jnp.concatenate([jnp.sin(angles), jnp.cos(angles)], axis=2)
    time_act = mish_value(embedded).astype(jnp.bfloat16).reshape(flat, 2 * half_dim)
    time_film = jnp.dot(time_act, w_time, preferred_element_type=jnp.float32)
    columns_in = columns(noisy_act).reshape(flat * horizon, -1)
    return (
        time_act,
        time_film,
        columns_in,
        noisy_act.reshape(flat * horizon, action_dims),
        noise.reshape(flat * horizon, action_dims),
        jnp.broadcast_to(advantage.reshape(flat, 1, 1), (flat, horizon, action_dims)).reshape(
            flat * horizon, action_dims
        ),
    )


def mish_both(values):
    small = jnp.exp(-jnp.abs(values))
    positive = values >= 0
    top = jnp.where(positive, 1.0 + 2.0 * small, small * (small + 2.0))
    bottom = top + jnp.where(positive, 2.0 * small * small, 2.0)
    inverse = 1.0 / (bottom * (1.0 + small))
    soft = top * (1.0 + small) * inverse
    sigmoid = jnp.where(positive, 1.0, small) * bottom * inverse
    return values * soft, soft + values * sigmoid * (1.0 - soft * soft)


def denoise_kernel(
    core_ref,
    film_ref,
    columns_ref,
    noisy_ref,
    noise_ref,
    weight_ref,
    time_ref,
    w_in_ref,
    w_mid_ref,
    w_res_ref,
    w_out_ref,
    kept_ref,
    sent_ref,
    film_grad_ref,
    first_ref,
    act_ref,
    slope_ref,
    second_ref,
    work_ref,
    taps_ref,
    grad_ref,
    mid_ref,
    packed_ref,
    sums_ref,
    more_ref,
    stat_ref,
    stats_ref,
    *,
    horizon,
):
    flat = film_ref.shape[0]
    channels = w_mid_ref.shape[1]
    action_dims = noise_ref.shape[1]
    group_size = channels // GROUPS
    count = group_size * horizon
    row_group = lax.broadcasted_iota(jnp.int32, (channels, channels), 0) // group_size
    lane_group = lax.broadcasted_iota(jnp.int32, (channels, channels), 1) // group_size
    same_group = (row_group == lane_group).astype(jnp.float32)
    step = lax.broadcasted_iota(jnp.int32, (horizon, channels), 0)

    def rows_of(f):
        return pl.ds(pl.multiple_of(f * horizon, horizon), horizon)

    def one(f):
        return pl.ds(f, 1)

    def group_mean(ref):
        return (
            jnp.dot(
                ref[...],
                same_group,
                precision=lax.Precision.HIGHEST,
                preferred_element_type=jnp.float32,
            )
            / count
        )

    def column_sum(values):
        return jnp.sum(values, axis=0, keepdims=True)

    def each(body):
        def run(f, carry):
            body(f)
            return carry

        lax.fori_loop(0, flat, run, 0)

    def shifted(values, distance):
        if distance == 0:
            return values
        rolled = pltpu.roll(values, (-distance) % horizon, 0)
        inside = jnp.logical_and(step + distance >= 0, step + distance < horizon)
        return jnp.where(inside, rolled, 0.0)

    def normalize(ref):
        def means(f):
            sums_ref[one(f), :] = column_sum(ref[rows_of(f), :])

        each(means)
        stat_ref[...] = group_mean(sums_ref)

        def squares(f):
            centred = ref[rows_of(f), :] - stat_ref[one(f), :]
            sums_ref[one(f), :] = column_sum(centred * centred)

        each(squares)
        stats_ref[...] = lax.rsqrt(group_mean(sums_ref) + 1e-05)

    first_ref[...] = jnp.dot(columns_ref[...], w_in_ref[...], preferred_element_type=jnp.float32)
    normalize(first_ref)
    first_inverse = stats_ref[...]

    def modulate(f):
        rows = rows_of(f)
        normed = (first_ref[rows, :] - stat_ref[one(f), :]) * stats_ref[one(f), :]
        act, slope = mish_both(normed)
        first_ref[rows, :] = normed
        act_ref[rows, :] = act
        slope_ref[rows, :] = slope
        modulated = film_ref[one(f), :channels] * act + film_ref[one(f), channels:]
        for tap in range(5):
            taps_ref[rows, tap * channels : (tap + 1) * channels] = shifted(
                modulated, tap - 2
            ).astype(jnp.bfloat16)

    each(modulate)

    second_ref[...] = jnp.dot(taps_ref[...], w_mid_ref[...], preferred_element_type=jnp.float32)
    normalize(second_ref)
    second_inverse = stats_ref[...]
    work_ref[...] = jnp.dot(noisy_ref[...], w_res_ref[...], preferred_element_type=jnp.float32)

    def activate(f):
        rows = rows_of(f)
        normed = (second_ref[rows, :] - stat_ref[one(f), :]) * stats_ref[one(f), :]
        act, slope = mish_both(normed)
        second_ref[rows, :] = normed
        grad_ref[rows, :] = (act + work_ref[rows, :]).astype(jnp.bfloat16)
        work_ref[rows, :] = slope

    each(activate)
    block_out = grad_ref[...]
    over_rows = (((0,), (0,)), ((), ()))
    over_lanes = (((1,), (1,)), ((), ()))
    errors = lax.dot_general(
        block_out, w_out_ref[...], over_lanes, preferred_element_type=jnp.float32
    )
    errors = errors - noise_ref[...].astype(jnp.float32)
    scale = 1.0 / (horizon * action_dims)
    err_sum = jnp.sum(jnp.sum(errors * errors, axis=1, keepdims=True), axis=0, keepdims=True)
    err_sum = err_sum * scale
    d_pred = (2.0 * weight_ref[...] * errors * scale).astype(jnp.bfloat16)
    grad_out = lax.dot_general(
        d_pred, block_out, over_rows, preferred_element_type=jnp.float32
    )
    d_block = jnp.dot(d_pred, w_out_ref[...], preferred_element_type=jnp.float32)
    grad_res = lax.dot_general(
        noisy_ref[...],
        d_block.astype(jnp.bfloat16),
        over_rows,
        preferred_element_type=jnp.float32,
    )
    work_ref[...] = work_ref[...] * d_block

    def back_sums(normed_ref):
        def sums(f):
            rows = rows_of(f)
            work = work_ref[rows, :]
            sums_ref[one(f), :] = column_sum(work)
            more_ref[one(f), :] = column_sum(work * normed_ref[rows, :])

        each(sums)

    def back(normed_ref, inverse):
        stat_ref[...] = group_mean(sums_ref) * inverse
        more_ref[...] = group_mean(more_ref) * inverse
        stats_ref[...] = inverse

        def apply(f):
            rows = rows_of(f)
            grad = work_ref[rows, :] * stats_ref[one(f), :] - stat_ref[one(f), :]
            grad = grad - normed_ref[rows, :] * more_ref[one(f), :]
            grad_ref[rows, :] = grad.astype(jnp.bfloat16)

        each(apply)

    back_sums(second_ref)
    back(second_ref, second_inverse)
    for tap in range(5):
        lanes = slice(tap * channels, (tap + 1) * channels)
        mid_ref[lanes, :] = lax.dot_general(
            taps_ref[:, lanes], grad_ref[...], over_rows, preferred_element_type=jnp.float32
        )

    for tap in range(5):
        second_ref[...] = lax.dot_general(
            grad_ref[...],
            w_mid_ref[tap * channels : (tap + 1) * channels, :],
            over_lanes,
            preferred_element_type=jnp.float32,
        )

        def add(f, tap=tap):
            rows = rows_of(f)
            piece = shifted(second_ref[rows, :], 2 - tap)
            if tap == 0:
                work_ref[rows, :] = piece
            else:
                work_ref[rows, :] = work_ref[rows, :] + piece

        each(add)

    def film_sums(f):
        rows = rows_of(f)
        grad = work_ref[rows, :]
        sums_ref[one(f), :] = column_sum(grad * act_ref[rows, :])
        more_ref[one(f), :] = column_sum(grad)
        work_ref[rows, :] = grad * film_ref[one(f), :channels] * slope_ref[rows, :]

    each(film_sums)
    d_film = jnp.concatenate([sums_ref[...], more_ref[...]], axis=1)
    samples = film_grad_ref.shape[0]
    film_grad_ref[...] = jnp.sum(d_film.reshape(samples, flat // samples, 2 * channels), axis=1)
    back_sums(first_ref)
    back(first_ref, first_inverse)
    grad_in = lax.dot_general(
        columns_ref[...], grad_ref[...], over_rows, preferred_element_type=jnp.float32
    )
    grad_time = lax.dot_general(
        time_ref[...],
        d_film.astype(jnp.bfloat16),
        over_rows,
        preferred_element_type=jnp.float32,
    )

    segments, groups, height, wide = kept_ref.shape
    lanes = wide // 2
    mid_rows, in_rows, side_rows, tall = layout_of(
        w_mid_ref.shape[0], w_in_ref.shape[0], w_res_ref.shape[0], time_ref.shape[1]
    )
    packed_ref[...] = jnp.zeros_like(packed_ref)
    err_row = jnp.broadcast_to(err_sum, (1, lanes))
    for s in range(segments):
        cols = slice(s * lanes, (s + 1) * lanes)
        packed_ref[s, :mid_rows, :] = jnp.concatenate(
            [mid_ref[:mid_rows, cols], mid_ref[mid_rows:, cols]], axis=1
        )
        packed_ref[s, mid_rows : mid_rows + w_in_ref.shape[0], :lanes] = grad_in[:, cols]
        packed_ref[s, mid_rows : mid_rows + action_dims, lanes:] = grad_res[:, cols]
        begin = mid_rows + side_rows
        packed_ref[s, begin : begin + action_dims, lanes:] = grad_out[:, cols]
        begin = begin + side_rows
        packed_ref[s, begin : begin + 1, lanes:] = err_row
        begin = mid_rows + in_rows
        packed_ref[s, begin:tall, :] = grad_time[:, s * wide : (s + 1) * wide]
    core = core_ref[0]
    for d in range(groups):
        mine = pl.ds(pl.multiple_of((2 * d + core) * height, 8), height)
        other = pl.ds(pl.multiple_of((2 * d + 1 - core) * height, 8), height)
        for s in range(segments):
            kept_ref[s, d] = packed_ref[s, mine, :]
            sent_ref[s, d] = packed_ref[s, other, :].astype(jnp.bfloat16)


def layout_of(mid, taps, action_dims, time):
    side_rows = -(-action_dims // 8) * 8
    in_rows = max(-(-taps // 8) * 8, 2 * side_rows + 8)
    return mid // 2, in_rows, side_rows, mid // 2 + in_rows + time


def load_kernel(*refs, blocks):
    sources, (gate_up_ref, down_ref, sems) = refs[: 4 * blocks], refs[4 * blocks :]
    loads = []
    for i, source in enumerate(sources):
        held = gate_up_ref if i < 2 * blocks else down_ref
        size = source.shape[0]
        place = held.at[pl.ds(i % (2 * blocks) * size, size)]
        loads.append(pltpu.make_async_copy(source, place, sems.at[i]))
    for load in loads:
        load.start()
    for load in loads:
        load.wait()


def trunk_kernel(order_ref, *refs, count, main, rest, fixed):
    row_refs, refs = refs[:count], refs[count:]
    gain_ref, gate_up_ref, down_ref = refs[:3]
    out_refs, (normed_ref, hidden_ref) = refs[3:-4], refs[-2:]
    parts, _, width = normed_ref.shape

    def place_of(k):
        return k if fixed else order_ref[k]

    start = 0
    for row_ref in row_refs:
        rows = row_ref.shape[0]
        wide = row_ref[...].astype(jnp.float32)
        factor = lax.rsqrt(jnp.mean(wide * wide, axis=1, keepdims=True) + 1e-05)
        normed = (wide * factor * gain_ref[...]).astype(jnp.bfloat16)
        for j in range(parts):
            normed_ref[j, start : start + rows, :] = normed[:, j * width : (j + 1) * width]
        start += rows

    def hide(i, carry):
        both = 0.0
        for k in range(parts):
            both = both + jnp.dot(
                normed_ref[place_of(k)],
                gate_up_ref[i * parts + k],
                preferred_element_type=jnp.float32,
            )
        if main:
            gate, up = both[:, :main], both[:, main : 2 * main]
            hidden_ref[i, :, :main] = (gate * jax.nn.sigmoid(gate) * up).astype(jnp.bfloat16)
        if rest:
            gate, up = both[:, 2 * main : 2 * main + rest], both[:, 2 * main + rest :]
            hidden_ref[i, :, main:] = (gate * jax.nn.sigmoid(gate) * up).astype(jnp.bfloat16)
        return carry

    lax.fori_loop(0, 2, hide, 0)

    def project(k, carry):
        piece = jnp.dot(hidden_ref[0], down_ref[k], preferred_element_type=jnp.float32)
        piece = piece + jnp.dot(
            hidden_ref[1], down_ref[parts + k], preferred_element_type=jnp.float32
        )
        begin = place_of(k) * width
        if not fixed:
            begin = pl.multiple_of(begin, LANES)
        start = 0
        for out_ref in out_refs:
            rows = out_ref.shape[0]
            out_ref[:, pl.ds(begin, width)] = piece[start : start + rows].astype(out_ref.dtype)
            start += rows
        return carry

    if fixed:
        for k in range(parts):
            project(k, 0)
    else:
        lax.fori_loop(0, parts, project, 0)


def split_hidden(values, parts, dim):
    width = values.shape[dim] // parts
    main = width // LANES * LANES
    rest = width - main
    blocks = []
    for j in range(parts):
        first = lax.slice_in_dim(values, j * main, (j + 1) * main, axis=dim)
        begin = parts * main + j * rest
        last = lax.slice_in_dim(values, begin, begin + rest, axis=dim)
        blocks.append((first, last))
    return blocks, main, rest


def body(
    trunk_in,
    norm_gain,
    w_gate,
    w_up,
    w_down,
    w_cond,
    w_time,
    w_in,
    w_mid,
    w_res,
    w_out,
    tsteps,
    advantage,
    actions,
    noise,
):
    segments = lax.axis_size("segment")
    segment_index = lax.axis_index("segment")
    core_index = lax.axis_index("mp")
    groups = lax.axis_size("dp")
    group_index = lax.axis_index("dp")
    is_first = segment_index == 0
    is_last = segment_index == segments - 1
    is_odd = segment_index % 2 == 1
    is_core = core_index == 1

    half = trunk_in.shape[1]
    width = 2 * half
    gain = norm_gain.astype(jnp.float32)
    micro_count = segments * REPEAT
    rows = trunk_in.shape[0] // (2 * micro_count)

    def ordered(own, other, axis):
        return jnp.where(
            is_core,
            jnp.concatenate([other, own], axis=axis),
            jnp.concatenate([own, other], axis=axis),
        )

    shares = trunk_in.reshape(micro_count, 2, rows, half)
    kept = lax.dynamic_index_in_dim(shares, core_index, 1, keepdims=False)
    traded = swap(lax.dynamic_index_in_dim(shares, 1 - core_index, 1, keepdims=False), "mp", 1)
    inputs = ordered(kept, traded, 2)

    local_samples = tsteps.shape[0]
    share = local_samples // segments
    own_rows = share // 2
    begin_row = segment_index * share + core_index * own_rows

    def own_part(values):
        return lax.dynamic_slice_in_dim(values, begin_row, own_rows, 0)

    gates, main, rest = split_hidden(w_gate[0], groups, 1)
    ups, _, _ = split_hidden(w_up[0], groups, 1)
    gate_up = jnp.stack(
        [jnp.concatenate([g[0], u[0], g[1], u[1]], axis=1) for g, u in zip(gates, ups)]
    )
    downs, _, _ = split_hidden(w_down[0], groups, 0)
    down = jnp.stack([jnp.concatenate(d, axis=0) for d in downs])

    def block(blocks, k):
        return lax.dynamic_slice_in_dim(blocks, group_index ^ k, 1, 0)

    near = [k for k in range(1, groups) if k & (k - 1) == 0]
    far = [k for k in range(1, groups) if k not in near]
    later = (inputs, w_cond, own_part(tsteps), own_part(advantage), own_part(actions), own_part(noise))
    if few("dp"):
        down_blocks = [block(down, k) for k in range(groups)]
        gate_blocks = [block(gate_up, k) for k in range(groups)]
        blocks = [list(pair) for pair in zip(gate_blocks, down_blocks)]
        got = {0: blocks[0]}
        for k in near:
            down_piece = swap(blocks[k][1], "dp", k)
            got[k] = [swap(blocks[k][0], "dp", k), down_piece]
    early = [gather(later[0][k], "dp") for k in range(LAG)]
    inputs = later[0]
    w_cond_other = swap(later[1], "mp", 1)
    prepared = prepare(*later[2:], w_time)
    if few("dp"):
        for k in far:
            got[k] = [swap(piece, "dp", k) for piece in blocks[k]]
        gate_ups = [got[k][0] for k in range(groups)]
        downs = [got[k][1] for k in range(groups)]
    else:
        gate_ups = [lax.all_to_all(gate_up, "dp", 0, 0, tiled=True)]
        downs = [lax.all_to_all(down, "dp", 0, 0, tiled=True)]
    gate_ups = gate_ups + [swap(piece, "mp", 1) for piece in gate_ups]
    downs = downs + [swap(piece, "mp", 1) for piece in downs]
    order = (group_index ^ jnp.arange(groups)).astype(jnp.int32)
    vmem = pl.BlockSpec(memory_space=pltpu.VMEM)
    gate_up_held, down_held = pl.pallas_call(
        functools.partial(load_kernel, blocks=len(gate_ups) // 2),
        out_shape=(
            pltpu.VMEM((2 * groups,) + gate_up.shape[1:], jnp.bfloat16),
            pltpu.VMEM((2 * groups,) + down.shape[1:], jnp.bfloat16),
        ),
        in_specs=[pl.BlockSpec(memory_space=pl.ANY)] * (2 * len(gate_ups)),
        out_specs=(vmem, vmem),
        scratch_shapes=[pltpu.SemaphoreType.DMA((2 * len(gate_ups),))],
        compiler_params=pltpu.CompilerParams(vmem_limit_bytes=TRUNK_VMEM),
        name="load",
    )(*gate_ups, *downs)
    order, w_cond_other, prepared, is_odd, is_first, is_last, is_core = lax.optimization_barrier(
        (order, w_cond_other, prepared, is_odd, is_first, is_last, is_core)
    )

    def layer(current, pieces, held):
        count = len(pieces)
        whole = pl.BlockSpec(memory_space=pltpu.VMEM)
        if few("dp"):
            shapes = [jax.ShapeDtypeStruct((rows, width), jnp.float32)]
            shapes += [jax.ShapeDtypeStruct((rows, width), jnp.bfloat16)] * (groups - 1)
        else:
            shapes = [jax.ShapeDtypeStruct((groups * rows, width), jnp.float32)]
        total = groups * rows
        shapes += [pltpu.VMEM(value.shape, value.dtype) for value in held]
        partial = pl.pallas_call(
            functools.partial(
                trunk_kernel, count=count, main=main, rest=rest, fixed=not few("dp")
            ),
            out_shape=shapes,
            in_specs=[pl.BlockSpec(memory_space=pltpu.SMEM)] + [whole] * (count + 3),
            out_specs=[whole] * len(shapes),
            scratch_shapes=[
                pltpu.VMEM((groups, total, width // groups), jnp.bfloat16),
                pltpu.VMEM((2, total, main + rest), jnp.bfloat16),
            ],
            compiler_params=pltpu.CompilerParams(vmem_limit_bytes=TRUNK_VMEM),
            input_output_aliases={count + 2: len(shapes) - 2, count + 3: len(shapes) - 1},
            name="trunk",
        )(order, *pieces, gain, *held)
        result = current.astype(jnp.float32)
        if few("dp"):
            result = result + partial[0]
            for k in range(1, groups):
                result = result + swap(partial[k], "dp", k).astype(jnp.float32)
        else:
            result = result + scatter_sum(partial[0], "dp", 0)
        return result.astype(jnp.bfloat16), partial[-2:]

    held = (gate_up_held, down_held)
    passed = {}
    finished = []
    slots = micro_count + LAG * (segments - 1)
    for slot in range(slots):
        current = inputs[slot] if slot < micro_count else None
        received = passed.pop(slot - LAG, None)
        if current is None:
            current = received
        elif received is not None:
            current = jnp.where(is_first, current, received)
        pieces = early[slot] if slot < LAG else gather(current, "dp")
        result, held = layer(current, pieces, held)
        if slot + LAG < slots and segments > 1:
            passed[slot] = hop(result, "segment", is_odd)
        if slot >= LAG * (segments - 1):
            finished.append(result)

    tokens = trunk_in.shape[0] // local_samples
    conds = []
    for result in finished:
        averaged = jnp.mean(result.astype(jnp.float32).reshape(-1, tokens, width), axis=1)
        conds.append(averaged.astype(jnp.bfloat16))
    conds = [
        jnp.concatenate(conds[i * REPEAT : (i + 1) * REPEAT], axis=0) for i in range(segments)
    ]
    cond = jnp.where(is_last, conds[-1], jnp.zeros_like(conds[-1]))
    for i in range(segments - 1):
        cond = cond + lax.ppermute(conds[i], "segment", [(segments - 1, i)])
    cond_act = mish_value(cond.astype(jnp.float32)).astype(jnp.bfloat16)
    act_kept = jnp.where(is_core, cond_act[:, half:], cond_act[:, :half])
    act_sent = jnp.where(is_core, cond_act[:, :half], cond_act[:, half:])
    film_cond = jnp.dot(act_kept, w_cond, preferred_element_type=jnp.float32)
    film_cond = film_cond + jnp.dot(act_sent, w_cond_other, preferred_element_type=jnp.float32)
    cond_kept = jnp.where(is_core, cond[:, half:], cond[:, :half])
    cond_sent = jnp.where(is_core, cond[:, :half], cond[:, half:])
    cond_wide = ordered(cond_kept, swap(cond_sent, "mp", 1), 0).astype(jnp.float32)
    act_half = mish_value(cond_wide).astype(jnp.bfloat16)
    time_act, time_film, columns_in, noisy, noise_rows, weights = prepared
    flat = time_act.shape[0]
    film = film_cond[:, None, :] + time_film.reshape(own_rows, -1, film_cond.shape[1])
    film = film.reshape(flat, -1)
    channels = w_mid.shape[1]
    lanes = channels // segments
    taps = w_in.shape[0]
    action_dims = w_res.shape[0]
    mid_rows, in_rows, side_rows, tall = layout_of(
        w_mid.shape[0], taps, action_dims, w_time.shape[0]
    )
    height = -(-tall // (16 * groups)) * 8
    rows_all = columns_in.shape[0]
    vmem = pl.BlockSpec(memory_space=pltpu.VMEM)
    block = (segments, groups, height, 2 * lanes)
    kept, traded, d_film_cond = pl.pallas_call(
        functools.partial(denoise_kernel, horizon=rows_all // flat),
        out_shape=(
            jax.ShapeDtypeStruct(block, jnp.float32),
            jax.ShapeDtypeStruct(block, jnp.bfloat16),
            jax.ShapeDtypeStruct((own_rows, 2 * channels), jnp.float32),
        ),
        in_specs=[pl.BlockSpec(memory_space=pltpu.SMEM)] + [vmem] * 10,
        out_specs=(vmem, vmem, vmem),
        scratch_shapes=[pltpu.VMEM((rows_all, channels), jnp.float32)] * 5
        + [
            pltpu.VMEM((rows_all, w_mid.shape[0]), jnp.bfloat16),
            pltpu.VMEM((rows_all, channels), jnp.bfloat16),
            pltpu.VMEM(w_mid.shape, jnp.float32),
            pltpu.VMEM((segments, 2 * groups * height, 2 * lanes), jnp.float32),
        ]
        + [pltpu.VMEM((flat, channels), jnp.float32)] * 4,
        compiler_params=pltpu.CompilerParams(vmem_limit_bytes=VMEM_LIMIT),
        name="denoise",
    )(
        core_index.astype(jnp.int32).reshape(1),
        film,
        columns_in,
        noisy,
        noise_rows,
        weights,
        time_act,
        w_in,
        w_mid,
        w_res,
        w_out.T,
    )
    film_own = d_film_cond.astype(jnp.bfloat16)
    film_all = ordered(film_own, swap(film_own, "mp", 1), 0)
    grad_cond = contract("sc,dc->sd", film_all, w_cond) * mish_slope(cond_wide)

    total = segments * groups
    part = (kept + swap(traded, "mp", 1).astype(jnp.float32)).astype(jnp.bfloat16)
    part = part.reshape(total, height, 2 * lanes)
    acts = jnp.broadcast_to(act_half.reshape(1, -1, 2 * lanes), (total, share * half // (2 * lanes), 2 * lanes))
    films = film_all.reshape(share, segments, 1, 2 * lanes).transpose(1, 2, 0, 3)
    films = jnp.broadcast_to(films, (segments, groups, share, 2 * lanes))
    films = films.reshape(total, share, 2 * lanes)
    got = lax.all_to_all(
        jnp.concatenate([part, acts, films], axis=1), ("segment", "dp"), 0, 0, tiled=True
    )
    split = height + acts.shape[1]
    part = jnp.sum(got[:, :height].astype(jnp.float32), axis=0).astype(jnp.bfloat16)
    summed = everywhere(part, ("dp", "mp"))
    acts = got[:, height:split].reshape(total * share, half)
    films = got[:, split:].reshape(total * share, 2 * lanes)
    grad_w_cond = contract("sd,sc->dc", acts, films)

    summed = summed.astype(jnp.float32)
    low, high = summed[:, :lanes], summed[:, lanes:]
    begin = mid_rows + 2 * side_rows
    loss = (high[begin, :1] / (groups * local_samples * tsteps.shape[1])).reshape(1)
    pieces = [
        jnp.concatenate([low[:mid_rows], high[:mid_rows]], axis=0),
        low[mid_rows : mid_rows + taps],
        high[mid_rows : mid_rows + action_dims],
        high[mid_rows + side_rows : mid_rows + side_rows + action_dims],
    ]
    grad_w_time = summed[mid_rows + in_rows : tall]
    return (
        pieces[1],
        pieces[0],
        pieces[2],
        pieces[3].T,
        grad_w_time,
        grad_w_cond,
        grad_cond,
        loss,
    )


def solution(mesh):
    in_specs = (
        P("dp", "mp"),
        P("segment", None),
        P("segment", "dp", "mp"),
        P("segment", "dp", "mp"),
        P("segment", "mp", "dp"),
        P("mp", None),
        P(),
        P(),
        P(),
        P(),
        P(),
        P("dp", None),
        P("dp", None),
        P("dp", None, None),
        P("dp", None, None, None),
    )
    out_specs = (
        P(None, "segment"),
        P(None, "segment"),
        P(None, "segment"),
        P("segment", None),
        P(None, "segment"),
        P("mp", "segment"),
        P(("dp", "segment"), "mp"),
        P(),
    )

    return jax.shard_map(body, mesh=mesh, in_specs=in_specs, out_specs=out_specs, check_vma=False)
```
